128 devices in a mesh: atom: 8 (over x, z_lo), row: 4 (over y), col: 4 (over z_hi, core).
Axes of the slice: x: 4, y: 4, z: 4 (z_hi: 2, z_lo: 2; z = z_hi * 2 + z_lo), core: 2. Of those that a mesh axis runs over, the one named last changes fastest.
Arguments:
- hyper_image: float32 [32, 64, 512], P(None, 'row', 'col'), may hold values from -6 to 6
- warm_codes: float32 [512, 64, 512], P('atom', 'row', 'col'), may hold values from -1.5 to 1.5
- dictionary: float32 [512, 9, 9, 32], P('atom'), may hold values from -6 to 6
- thresholds: float32 [512], P('atom'), may hold values from 0.5 to 5
- velocity: float32 [512, 9, 9, 32], P(('atom', 'row', 'col')), may hold values from -0.012 to 0.012
Outputs:
- new_codes: float32 [512, 64, 512], P('atom', 'row', 'col')
- new_atoms: float32 [512, 9, 9, 32], P(('atom', 'row', 'col'))
- new_velocity: float32 [512, 9, 9, 32], P(('atom', 'row', 'col'))
The draws below stay inside these ranges and needn't reach their ends.
All inputs are finite; a program needn't handle non-finite values.
Results may differ from the reference program's by a relative error of at most 0.0003.
Values sent between devices are 32-bit elements; how exact they have to be, the bound alone decides.
A program may use at most 64 MiB of HBM per device.

```python
import math
import jax
import jax.numpy as jnp
from jax import lax

K = 512
C = 32
SIDE = 9
ITERS = 2
H = 64
W = 512


def levels(key, dims, cuts, least, top_value):
    def one(position, shards_of):
        steps = jax.random.uniform(jax.random.fold_in(jax.random.fold_in(key, 6), position), (shards_of,), jnp.float32, least / len(cuts), top_value / len(cuts))
        return jnp.repeat(jnp.exp(steps), dims[position] // shards_of).reshape((-1,) + (1,) * (len(dims) - position - 1))

    level = one(*cuts[0])
    for cut in cuts[1:]:
        level = level * one(*cut)
    return level


def normal_values(stream_key, extent, deviation, limit, pieces=(), kind=jnp.bfloat16):
    drawn = jax.random.normal(stream_key, extent, jnp.float32) * deviation
    if len(pieces) > 0:
        drawn = levels(stream_key, extent, pieces, -0.22, 0.18) * drawn
    return jnp.clip(drawn, min=-limit, max=limit).astype(kind)


def setup_inputs(seed: int = 0) -> dict:
    arg_keys = jax.random.split(jax.random.key(seed), 6)
    return {
        "hyper_image": normal_values(arg_keys[0], (C, H, W), 1.0, 6.0, ((1, 4), (2, 4)), jnp.float32),
        "warm_codes": normal_values(arg_keys[1], (K, H, W), 0.25, 1.5, ((0, 8), (1, 4), (2, 4)), jnp.float32),
        "dictionary": normal_values(arg_keys[2], (K, SIDE, SIDE, C), 1.0, 6.0, ((0, 8),), jnp.float32),
        "thresholds": jnp.clip(jnp.exp(math.log(5.0) - 2.3025851 * jax.random.uniform(arg_keys[3], (K,), jnp.float32) ** levels(arg_keys[3], (K,), ((0, 8),), -0.2, 0.2)), 0.5, 5.0),
        "velocity": normal_values(arg_keys[4], (K, SIDE, SIDE, C), 0.002, 0.012, ((0, 128),), jnp.float32),
    }


PRECISION_HIGH = lax.Precision.HIGHEST
ETA_CODE = 0.05
MOMENTUM = 0.9
LEARN_RATE = 200.0
EPSILON = 1e-06

def forward_image(padded, dictionary):
    atom_side = dictionary.shape[1]
    row_count = padded.shape[1] - atom_side + 1
    col_count = padded.shape[2] - atom_side + 1
    channels = dictionary.shape[3]

    def row_step(offset_row, accumulated):
        strip_rows = lax.dynamic_slice_in_dim(padded, offset_row, row_count, 1)
        tap_row = lax.dynamic_index_in_dim(dictionary, offset_row, 1, keepdims=False)
        for offset_col in range(atom_side):
            accumulated = accumulated + jnp.einsum('kc,khw->chw', tap_row[:, offset_col, :], strip_rows[:, :, offset_col:offset_col + col_count], precision=PRECISION_HIGH, preferred_element_type=jnp.float32)
        return accumulated
    initial = jnp.zeros((channels, row_count, col_count), jnp.float32)
    accumulated = lax.fori_loop(0, atom_side, row_step, initial)
    return accumulated * (1.0 / math.sqrt(atom_side * atom_side * channels))

def adjoint_map(padded_err, dictionary):
    atom_side = dictionary.shape[1]
    margin = atom_side - 1
    row_count = padded_err.shape[1] - margin
    col_count = padded_err.shape[2] - margin
    channels = dictionary.shape[3]

    def row_step(offset_row, accumulated):
        strip_rows = lax.dynamic_slice_in_dim(padded_err, margin - offset_row, row_count, 1)
        tap_row = lax.dynamic_index_in_dim(dictionary, offset_row, 1, keepdims=False)
        for offset_col in range(atom_side):
            accumulated = accumulated + jnp.einsum('kc,chw->khw', tap_row[:, offset_col, :], strip_rows[:, :, margin - offset_col:margin - offset_col + col_count], precision=PRECISION_HIGH, preferred_element_type=jnp.float32)
        return accumulated
    initial = jnp.zeros((dictionary.shape[0], row_count, col_count), jnp.float32)
    accumulated = lax.fori_loop(0, atom_side, row_step, initial)
    return accumulated * (1.0 / math.sqrt(atom_side * atom_side * channels))

def correlate(error_field, padded_codes, first_row, row_total, atom_side):
    row_count = error_field.shape[1]
    col_count = error_field.shape[2]
    chosen = lax.dynamic_slice_in_dim(padded_codes, first_row, row_total, 0)
    tap_terms = []
    for offset_row in range(atom_side):
        for offset_col in range(atom_side):
            tap_terms.append(jnp.einsum('chw,khw->kc', error_field, chosen[:, offset_row:offset_row + row_count, offset_col:offset_col + col_count], precision=PRECISION_HIGH, preferred_element_type=jnp.float32))
    stacked = jnp.stack(tap_terms, axis=1)
    return stacked.reshape(row_total, atom_side, atom_side, error_field.shape[0])

def shrink_step(code_field, gradient, thresholds):
    shifted_codes = code_field - ETA_CODE * gradient
    threshold_level = ETA_CODE * thresholds[:, None, None]
    return jnp.sign(shifted_codes) * jnp.maximum(jnp.abs(shifted_codes) - threshold_level, 0.0)

def pad_field(code_field, rim_width):
    return jnp.pad(code_field, ((0, 0), (rim_width, rim_width), (rim_width, rim_width)))

def reference(hyper_image, warm_codes, dictionary, thresholds, velocity):
    atom_side = dictionary.shape[1]
    rim_width = atom_side // 2
    current = warm_codes
    for iteration in range(ITERS):
        padded_codes = pad_field(current, rim_width)
        error_field = forward_image(padded_codes, dictionary) - hyper_image
        gradient = adjoint_map(pad_field(error_field, rim_width), dictionary)
        current = shrink_step(current, gradient, thresholds)
    padded_codes = pad_field(current, rim_width)
    error_field = forward_image(padded_codes, dictionary) - hyper_image
    summed = correlate(error_field, padded_codes, 0, dictionary.shape[0], atom_side)
    pixels = error_field.shape[1] * error_field.shape[2]
    new_velocity = MOMENTUM * velocity + summed / pixels
    stepped = dictionary - LEARN_RATE * new_velocity
    mean_square = lax.optimization_barrier(jnp.mean(stepped * stepped, axis=(1, 2, 3), keepdims=True))
    new_atoms = stepped * lax.rsqrt(mean_square + EPSILON)
    return (current, new_atoms, new_velocity)
```

```python
import functools
import math

import jax
import jax.numpy as jnp
from jax import lax
from jax.experimental import pallas as pl
from jax.experimental.pallas import tpu as pltpu
from jax.sharding import PartitionSpec as P

ITERS = 2
ETA_CODE = 0.05
MOMENTUM = 0.9
LEARN_RATE = 200.0
EPSILON = 1e-06

F32 = jnp.float32
BF16 = jnp.bfloat16
MESH = pl.DeviceIdType.MESH
VMEM = pl.BlockSpec(memory_space=pltpu.VMEM)
ANY = pl.BlockSpec(memory_space=pl.ANY)

C = 32
T = 9
KL = 64
ROWS = 16
LANES = 128
EXT = ROWS + 8
SLOTS = EXT + 2
SCALE = 1.0 / math.sqrt(T * T * C)


def split(x):
    hi = x.astype(BF16)
    return hi, (x - hi.astype(F32)).astype(BF16)


def lane_index(rows):
    return lax.broadcasted_iota(jnp.int32, (rows, LANES), 1)


def roll(x, shift):
    return pltpu.roll(x, shift % LANES, 1) if shift % LANES else x


def inside(lane, shift):
    return lane >= shift if shift > 0 else lane < LANES + shift


def synthesis(codes, ws, zbuf, acc, part):
    owners = part.shape[0]
    share = C // owners
    lane = lane_index(C)
    zero_rows = jnp.zeros((3 * KL, 2 * LANES), BF16)
    zbuf[0 : 3 * KL] = zero_rows
    zbuf[9 * 3 * KL : 10 * 3 * KL] = zero_rows
    for t in range(8):
        hi, lo = split(jnp.concatenate([codes[t], codes[t + 8]], axis=1))
        base = (t + 1) * 3 * KL
        zbuf[base : base + KL] = hi
        zbuf[base + KL : base + 2 * KL] = lo
        zbuf[base + 2 * KL : base + 3 * KL] = hi
    rims = [jnp.zeros((C, LANES), F32), jnp.zeros((C, LANES), F32)]

    def put(slot, row):
        for q in range(owners):
            part[q, slot] = row[q * share : (q + 1) * share]

    for ho in range(16):
        first, last = max(0, 8 - ho) // 2, min(8, 15 - ho) // 2
        depth = (last - first + 1) * 6 * KL
        start = (2 * first + ho - 7) * 3 * KL
        taps = jnp.dot(
            ws[:, first * 6 * KL : first * 6 * KL + depth],
            zbuf[start : start + depth],
            preferred_element_type=F32,
        )
        for half in range(2):
            main = jnp.zeros((C, LANES), F32)
            rim = jnp.zeros((C, LANES), F32)
            for b in range(T):
                moved = roll(taps[b * C : (b + 1) * C, half * LANES : (half + 1) * LANES], 4 - b)
                if b == 4:
                    main = main + moved
                else:
                    keep = inside(lane, 4 - b)
                    main = main + jnp.where(keep, moved, 0.0)
                    rim = rim + jnp.where(keep, 0.0, moved)
            row = ho + 8 * half
            rims[row // 16] = rims[row // 16] + roll(rim, 8 * (row % 16) + 4)
            if half == 0 and ho >= 8:
                main = main + acc[ho - 8]
            if half == 1 and ho < 8:
                acc[ho] = main
            else:
                put(row + 1, main)
    put(0, rims[0])
    put(SLOTS - 1, rims[1])


def gathered(err, slot):
    return jnp.concatenate([err[q, slot] for q in range(err.shape[0])], axis=0)


def adjoint_step(err, wa, level, codes, ebuf, hbuf, qbuf, gbuf, new_codes):
    wide = 3 * C
    lane_c = lane_index(C)
    lane = lane_index(KL)
    spot = lane % 8
    for row in range(EXT):
        hi, lo = split(gathered(err, row + 1))
        for t, side in ((row, 0), (row - 8, 1)):
            if 0 <= t < 16:
                cols = slice(side * LANES, (side + 1) * LANES)
                ebuf[t * wide : t * wide + C, cols] = hi
                ebuf[t * wide + C : t * wide + 2 * C, cols] = lo
                ebuf[t * wide + 2 * C : t * wide + 3 * C, cols] = hi
    rims = [gathered(err, 0), gathered(err, SLOTS - 1)]
    for t in range(T):
        hi, lo = split(
            jnp.where(lane_c < LANES - 8 * t, roll(rims[0], -8 * t), roll(rims[1], -8 * t))
        )
        hbuf[t * wide : t * wide + C] = hi
        hbuf[t * wide + C : t * wide + 2 * C] = lo
        hbuf[t * wide + 2 * C : t * wide + 3 * C] = hi
    qbuf[:, 0:LANES] = jnp.dot(wa[...], hbuf[...], preferred_element_type=F32)
    edge = jnp.zeros((KL, LANES), F32)
    for b in range(T):
        s = b - 4
        if s == 0:
            continue
        keep = (spot >= 4) & (spot < 4 + s) if s > 0 else (spot < 4) & (spot >= 4 + s)
        edge = edge + jnp.where(keep, roll(qbuf[b * KL : (b + 1) * KL, 0:LANES], s), 0.0)
    gbuf[...] = edge
    ends = (lane < 4) | (lane >= LANES - 4)
    bound = level[...]
    for i in range(8):
        qbuf[...] = jnp.dot(
            wa[...], ebuf[i * wide : (i + T) * wide], preferred_element_type=F32
        )
        for half in range(2):
            row = i + 8 * half
            total = jnp.where(ends, roll(gbuf[...], -(8 * row + 4)), 0.0)
            for b in range(T):
                moved = roll(qbuf[b * KL : (b + 1) * KL, half * LANES : (half + 1) * LANES], b - 4)
                if b != 4:
                    moved = jnp.where(inside(lane, b - 4), moved, 0.0)
                total = total + moved
            shifted = codes[row] - (ETA_CODE * SCALE) * total
            new_codes[row] = shifted - jnp.clip(shifted, -bound, bound)


def correlation(err, codes, lbuf, cbuf, gacc, parts):
    lane = lane_index(C)
    rims = [gathered(err, 0), gathered(err, SLOTS - 1)]
    for row in range(EXT):
        main = gathered(err, row + 1)
        rim = roll(rims[row // 16], -(8 * (row % 16) + 4))
        for b in range(T):
            s = b - 4
            if s > 0:
                field = jnp.where(lane >= LANES - s, rim, main)
            elif s < 0:
                field = jnp.where(lane < -s, rim, main)
            else:
                field = main
            hi, lo = split(roll(field, s))
            at = row * 3 * LANES
            lbuf[b * C : (b + 1) * C, at : at + LANES] = hi
            lbuf[b * C : (b + 1) * C, at + LANES : at + 2 * LANES] = hi
            lbuf[b * C : (b + 1) * C, at + 2 * LANES : at + 3 * LANES] = lo
    none = jnp.zeros((KL, 3 * LANES), BF16)
    cbuf[0:KL, 0 : 3 * LANES] = none
    cbuf[ROWS * KL : (ROWS + 1) * KL, 3 * LANES : 6 * LANES] = none
    for i in range(ROWS):
        hi, lo = split(codes[i])
        for at, base in (((i + 1) * KL, 0), (i * KL, 3 * LANES)):
            cbuf[at : at + KL, base : base + LANES] = hi
            cbuf[at : at + KL, base + LANES : base + 2 * LANES] = lo
            cbuf[at : at + KL, base + 2 * LANES : base + 3 * LANES] = hi
    gacc[...] = jnp.zeros_like(gacc)
    for row in range(0, EXT, 2):
        low, high = max(row - 8, -1), min(row, ROWS - 1)
        a = low - row + 8
        count = (high - low + 1) * KL
        gacc[a * KL : a * KL + count] += lax.dot_general(
            cbuf[(low + 1) * KL : (low + 1) * KL + count],
            lbuf[:, row * 3 * LANES : (row + 2) * 3 * LANES],
            (((1,), (1,)), ((), ())),
            preferred_element_type=F32,
        )
    groups, share = parts.shape[1], parts.shape[3]
    for core in range(2):
        for g in range(groups):
            for a in range(T):
                at = a * KL + (2 * g + core) * share
                parts[core, g, a] = gacc[at : at + share]


def first_kernel(warm, ws, codes, part, zbuf, acc, sem):
    copies = [pltpu.make_async_copy(warm.at[:, i], codes.at[i], sem.at[i]) for i in range(ROWS)]
    for copy in copies:
        copy.start()
    for copy in copies:
        copy.wait()
    synthesis(codes, ws, zbuf, acc, part)


def step_kernel(err, wa, ws, level, codes, new_codes, part, ebuf, hbuf, qbuf, gbuf, zbuf, acc):
    adjoint_step(err, wa, level, codes, ebuf, hbuf, qbuf, gbuf, new_codes)
    synthesis(new_codes, ws, zbuf, acc, part)


def last_kernel(err, codes, out, parts, lbuf, cbuf, gacc, sem):
    copies = [pltpu.make_async_copy(codes.at[i], out.at[:, i], sem.at[i]) for i in range(ROWS)]
    for copy in copies:
        copy.start()
    correlation(err, codes, lbuf, cbuf, gacc, parts)
    for copy in copies:
        copy.wait()


def greet(peers):
    barrier = pltpu.get_barrier_semaphore()
    for peer in peers:
        pl.semaphore_signal(barrier, inc=1, device_id=peer, device_id_type=MESH)
    pl.semaphore_wait(barrier, len(peers))


def send(src, dst, sems, slot, peer):
    copy = pltpu.make_async_remote_copy(
        src_ref=src,
        dst_ref=dst,
        send_sem=sems.at[0, slot],
        recv_sem=sems.at[1, slot],
        device_id=peer,
        device_id_type=MESH,
    )
    copy.start()
    return copy


def wait_all(copies):
    for copy in copies:
        copy.wait_recv()
    for copy in copies:
        copy.wait_send()


def exchange_kernel(
    sizes, part, image, err, rbuf, piece, piece2, h1, msg, h2, field, s_rs, s_h1, s_h2, s_ag
):
    owners, rows, cols = sizes
    share = C // owners
    q, r, c = lax.axis_index("atom"), lax.axis_index("row"), lax.axis_index("col")
    others = [{"atom": lax.rem(q + d, owners)} for d in range(1, owners)]
    up, down = {"row": lax.rem(r + rows - 1, rows)}, {"row": lax.rem(r + 1, rows)}
    left, right = {"col": lax.rem(c + cols - 1, cols)}, {"col": lax.rem(c + 1, cols)}
    greet(others + [up, down, left, right])

    wait_all(
        [send(part.at[p["atom"]], rbuf.at[d], s_rs, d, p) for d, p in enumerate(others)]
    )
    total = part[q]
    for d in range(owners - 1):
        total = total + rbuf[d]
    total = total * SCALE
    piece[0:5] = total[0:5]
    piece[5:21] = total[5:21] - image[...]
    piece[21:SLOTS] = total[21:SLOTS]

    f_up, f_down = (r > 0).astype(F32), (r < rows - 1).astype(F32)
    f_left, f_right = (c > 0).astype(F32), (c < cols - 1).astype(F32)
    lane = lane_index(share)
    wait_all(
        [
            send(piece.at[17:26], h1.at[0], s_h1, 0, down),
            send(piece.at[0:9], h1.at[1], s_h1, 1, up),
        ]
    )
    piece2[0] = piece[0] + h1[0, 8] * f_up
    piece2[1:9] = piece[1:9] + h1[0, 0:8] * f_up
    piece2[9:17] = piece[9:17]
    piece2[17:25] = piece[17:25] + h1[1, 1:9] * f_down
    piece2[25] = piece[25] + jnp.where(lane < 64, h1[1, 0], 0.0) * f_down

    ends = (lane < 4) | (lane >= LANES - 4)
    low = lane % 8 < 4
    packed = [jnp.zeros((share, LANES), F32), jnp.zeros((share, LANES), F32)]
    for row in range(EXT):
        packed[row // 16] += roll(jnp.where(ends, piece2[row + 1], 0.0), 8 * (row % 16) + 4)
    rims = [piece2[0], piece2[SLOTS - 1]]
    for v in range(2):
        msg[0, v] = jnp.where(low, packed[v], rims[v])
        msg[1, v] = jnp.where(low, rims[v], packed[v])
    wait_all(
        [
            send(msg.at[0], h2.at[0], s_h2, 0, right),
            send(msg.at[1], h2.at[1], s_h2, 1, left),
        ]
    )
    inner = [None, None]
    for v in range(2):
        from_left, from_right = h2[0, v] * f_left, h2[1, v] * f_right
        rims[v] = rims[v] + jnp.where(low, from_left, from_right)
        inner[v] = jnp.where(low, from_right, from_left)
        rims[v] = rims[v] * jnp.where(low, f_left, f_right)
    for row in range(EXT):
        fix = roll(inner[row // 16], -(8 * (row % 16) + 4))
        value = piece2[row + 1] + jnp.where(ends, fix, 0.0)
        if row < 4:
            value = value * f_up
        if row >= EXT - 4:
            value = value * f_down
        field[row + 1] = value
    field[0] = rims[0] * jnp.where(lane < 32, f_up, 1.0)
    field[SLOTS - 1] = jnp.where(lane < 64, rims[1] * jnp.where(lane >= 32, f_down, 1.0), 0.0)

    copies = [send(field, err.at[q], s_ag, d, p) for d, p in enumerate(others)]
    err[q] = field[...]
    wait_all(copies)


def update_kernel(sizes, parts, atoms, velocity, new_atoms, new_velocity, half, total, chunks, s1, s2):
    rows, halves = sizes
    r, c = lax.axis_index("row"), lax.axis_index("col")
    core, z = lax.rem(c, 2), lax.div(c, 2)
    partner = {"col": 2 * z + 1 - core}
    others = []
    for dr in range(rows):
        for dz in range(halves):
            if dr + dz > 0:
                pr, pz = lax.rem(r + dr, rows), lax.rem(z + dz, halves)
                others.append((pr * halves + pz, {"row": pr, "col": 2 * pz + core}))
    greet([partner] + [p for _, p in others])
    wait_all([send(parts.at[1 - core], half, s1, 0, partner)])
    total[...] = parts[core] + half[...]
    wait_all([send(total.at[g], chunks.at[d], s2, d, p) for d, (g, p) in enumerate(others)])
    summed = total[r * halves + z]
    for d in range(len(others)):
        summed = summed + chunks[d]
    pixels = ROWS * LANES * rows * halves * 2
    fresh = MOMENTUM * velocity[...] + summed * (1.0 / pixels)
    stepped = atoms[...] - LEARN_RATE * fresh
    square = jnp.sum(jnp.sum(stepped * stepped, axis=0), axis=1, keepdims=True) * (1.0 / (T * T * C))
    new_velocity[...] = fresh
    new_atoms[...] = stepped * lax.rsqrt(square + EPSILON)[None]


def struct(shape, dtype=F32):
    return jax.ShapeDtypeStruct(shape, dtype)


def params(collective_id=None):
    if collective_id is None:
        return pltpu.CompilerParams(vmem_limit_bytes=60 << 20)
    return pltpu.CompilerParams(
        vmem_limit_bytes=60 << 20, collective_id=collective_id, has_side_effects=True
    )


def shards(hyper_image, warm_codes, dictionary, thresholds, velocity):
    owners, rows, cols = lax.axis_size("atom"), lax.axis_size("row"), lax.axis_size("col")
    share, owned, halves = C // owners, velocity.shape[0], cols // 2
    q = lax.axis_index("atom")

    hi = lax.reduce_precision(dictionary, 8, 7)
    lo = (dictionary - hi).astype(BF16)
    hi = hi.astype(BF16)
    triple = jnp.stack([hi, hi, lo])
    ws = triple.transpose(3, 4, 2, 0, 1).reshape(T * C, T * 3 * KL)
    ws = jnp.pad(ws, ((0, 0), (0, 3 * KL)))
    wa = triple[:, :, ::-1].transpose(3, 1, 2, 0, 4).reshape(T * KL, T * 3 * C)
    level = jnp.broadcast_to((ETA_CODE * thresholds)[:, None], (KL, LANES))
    image = lax.dynamic_slice_in_dim(hyper_image, q * share, share, 0).transpose(1, 0, 2)

    code_shape, part_shape = (ROWS, KL, LANES), (owners, SLOTS, share, LANES)
    synth_scratch = [
        pltpu.VMEM((10 * 3 * KL, 2 * LANES), BF16),
        pltpu.VMEM((8, C, LANES), F32),
    ]
    codes, part = pl.pallas_call(
        first_kernel,
        out_shape=(struct(code_shape), struct(part_shape)),
        in_specs=[ANY, VMEM],
        out_specs=(VMEM, VMEM),
        scratch_shapes=synth_scratch + [pltpu.SemaphoreType.DMA((ROWS,))],
        compiler_params=params(),
    )(warm_codes, ws)

    def exchange(part):
        piece = pltpu.VMEM((SLOTS, share, LANES), F32)
        return pl.pallas_call(
            functools.partial(exchange_kernel, (owners, rows, cols)),
            out_shape=struct(part_shape),
            in_specs=[VMEM, VMEM],
            out_specs=VMEM,
            scratch_shapes=[
                pltpu.VMEM((owners - 1, SLOTS, share, LANES), F32),
                piece,
                piece,
                pltpu.VMEM((2, 9, share, LANES), F32),
                pltpu.VMEM((2, 2, share, LANES), F32),
                pltpu.VMEM((2, 2, share, LANES), F32),
                piece,
                pltpu.SemaphoreType.DMA((2, owners - 1)),
                pltpu.SemaphoreType.DMA((2, 2)),
                pltpu.SemaphoreType.DMA((2, 2)),
                pltpu.SemaphoreType.DMA((2, owners - 1)),
            ],
            compiler_params=params(0),
        )(part, image)

    for _ in range(ITERS):
        err = exchange(part)
        codes, part = pl.pallas_call(
            step_kernel,
            out_shape=(struct(code_shape), struct(part_shape)),
            in_specs=[VMEM] * 5,
            out_specs=(VMEM, VMEM),
            scratch_shapes=[
                pltpu.VMEM((16 * 3 * C, 2 * LANES), BF16),
                pltpu.VMEM((T * 3 * C, LANES), BF16),
                pltpu.VMEM((T * KL, 2 * LANES), F32),
                pltpu.VMEM((KL, LANES), F32),
            ]
            + synth_scratch,
            compiler_params=params(),
        )(err, wa, ws, level, codes)
    err = exchange(part)

    new_codes, parts = pl.pallas_call(
        last_kernel,
        out_shape=(
            struct((KL, ROWS, LANES)),
            struct((2, rows * halves, T, owned, T * C)),
        ),
        in_specs=[VMEM, VMEM],
        out_specs=(ANY, VMEM),
        scratch_shapes=[
            pltpu.VMEM((T * C, EXT * 3 * LANES), BF16),
            pltpu.VMEM(((ROWS + 1) * KL, 6 * LANES), BF16),
            pltpu.VMEM((T * KL, T * C), F32),
            pltpu.SemaphoreType.DMA((ROWS,)),
        ],
        compiler_params=params(),
    )(err, codes)

    start = (lax.axis_index("row") * cols + lax.axis_index("col")) * owned

    def flat(block):
        return block.transpose(1, 0, 2, 3).reshape(T, owned, T * C)

    def unflat(block):
        return block.reshape(T, owned, T, C).transpose(1, 0, 2, 3)

    piece_shape = (T, owned, T * C)
    new_atoms, new_velocity = pl.pallas_call(
        functools.partial(update_kernel, (rows, halves)),
        out_shape=(struct(piece_shape), struct(piece_shape)),
        in_specs=[VMEM] * 3,
        out_specs=(VMEM, VMEM),
        scratch_shapes=[
            pltpu.VMEM((rows * halves,) + piece_shape, F32),
            pltpu.VMEM((rows * halves,) + piece_shape, F32),
            pltpu.VMEM((rows * halves - 1,) + piece_shape, F32),
            pltpu.SemaphoreType.DMA((2, 1)),
            pltpu.SemaphoreType.DMA((2, rows * halves - 1)),
        ],
        compiler_params=params(1),
    )(
        parts,
        flat(lax.dynamic_slice_in_dim(dictionary, start, owned, 0)),
        flat(velocity),
    )
    return new_codes, unflat(new_atoms), unflat(new_velocity)


def solution(mesh):
    in_specs = (
        P(None, "row", "col"),
        P("atom", "row", "col"),
        P("atom", None, None, None),
        P("atom"),
        P(("atom", "row", "col"), None, None, None),
    )
    out_specs = (
        P("atom", "row", "col"),
        P(("atom", "row", "col"), None, None, None),
        P(("atom", "row", "col"), None, None, None),
    )
    return jax.shard_map(shards, mesh=mesh, in_specs=in_specs, out_specs=out_specs, check_vma=False)
```

```python
import functools
import math

import jax
import jax.numpy as jnp
from jax import lax
from jax.experimental import pallas as pl
from jax.experimental.pallas import tpu as pltpu
from jax.sharding import PartitionSpec as P

ITERS = 2
ETA_CODE = 0.05
MOMENTUM = 0.9
LEARN_RATE = 200.0
EPSILON = 1e-06

F32 = jnp.float32
BF16 = jnp.bfloat16
MESH = pl.DeviceIdType.MESH
VMEM = pl.BlockSpec(memory_space=pltpu.VMEM)
ANY = pl.BlockSpec(memory_space=pl.ANY)

C = 32
T = 9
KL = 64
ROWS = 16
LANES = 128
EXT = ROWS + 8
SLOTS = EXT + 2
SCALE = 1.0 / math.sqrt(T * T * C)


def split(x):
    hi = x.astype(BF16)
    return hi, (x - hi.astype(F32)).astype(BF16)


def lane_index(rows):
    return lax.broadcasted_iota(jnp.int32, (rows, LANES), 1)


def roll(x, shift):
    return pltpu.roll(x, shift % LANES, 1) if shift % LANES else x


def inside(lane, shift):
    return lane >= shift if shift > 0 else lane < LANES + shift


def synthesis(codes, ws, zbuf, acc, part):
    owners = part.shape[0]
    share = C // owners
    lane = lane_index(C)
    zero_rows = jnp.zeros((3 * KL, 2 * LANES), BF16)
    zbuf[0 : 3 * KL] = zero_rows
    zbuf[9 * 3 * KL : 10 * 3 * KL] = zero_rows
    for t in range(8):
        hi, lo = split(jnp.concatenate([codes[t], codes[t + 8]], axis=1))
        base = (t + 1) * 3 * KL
        zbuf[base : base + KL] = hi
        zbuf[base + KL : base + 2 * KL] = lo
        zbuf[base + 2 * KL : base + 3 * KL] = hi
    rims = [jnp.zeros((C, LANES), F32), jnp.zeros((C, LANES), F32)]

    def put(slot, row):
        for q in range(owners):
            part[q, slot] = row[q * share : (q + 1) * share]

    for ho in range(16):
        first, last = max(0, 8 - ho) // 2, min(8, 15 - ho) // 2
        depth = (last - first + 1) * 6 * KL
        start = (2 * first + ho - 7) * 3 * KL
        taps = jnp.dot(
            ws[:, first * 6 * KL : first * 6 * KL + depth],
            zbuf[start : start + depth],
            preferred_element_type=F32,
        )
        for half in range(2):
            main = jnp.zeros((C, LANES), F32)
            rim = jnp.zeros((C, LANES), F32)
            for b in range(T):
                moved = roll(taps[b * C : (b + 1) * C, half * LANES : (half + 1) * LANES], 4 - b)
                if b == 4:
                    main = main + moved
                else:
                    keep = inside(lane, 4 - b)
                    main = main + jnp.where(keep, moved, 0.0)
                    rim = rim + jnp.where(keep, 0.0, moved)
            row = ho + 8 * half
            rims[row // 16] = rims[row // 16] + roll(rim, 8 * (row % 16) + 4)
            if half == 0 and ho >= 8:
                main = main + acc[ho - 8]
            if half == 1 and ho < 8:
                acc[ho] = main
            else:
                put(row + 1, main)
    put(0, rims[0])
    put(SLOTS - 1, rims[1])


def gathered(err, slot):
    return jnp.concatenate([err[q, slot] for q in range(err.shape[0])], axis=0)


def adjoint_step(err, wa, level, codes, ebuf, hbuf, qbuf, gbuf):
    wide = 3 * C
    lane_c = lane_index(C)
    lane = lane_index(KL)
    spot = lane % 8
    for row in range(EXT):
        hi, lo = split(gathered(err, row + 1))
        for t, side in ((row, 0), (row - 8, 1)):
            if 0 <= t < 16:
                cols = slice(side * LANES, (side + 1) * LANES)
                ebuf[t * wide : t * wide + C, cols] = hi
                ebuf[t * wide + C : t * wide + 2 * C, cols] = lo
                ebuf[t * wide + 2 * C : t * wide + 3 * C, cols] = hi
    rims = [gathered(err, 0), gathered(err, SLOTS - 1)]
    for t in range(T):
        hi, lo = split(
            jnp.where(lane_c < LANES - 8 * t, roll(rims[0], -8 * t), roll(rims[1], -8 * t))
        )
        hbuf[t * wide : t * wide + C] = hi
        hbuf[t * wide + C : t * wide + 2 * C] = lo
        hbuf[t * wide + 2 * C : t * wide + 3 * C] = hi
    qbuf[:, 0:LANES] = jnp.dot(wa[:, 0 : T * wide], hbuf[...], preferred_element_type=F32)
    edge = jnp.zeros((KL, LANES), F32)
    for b in range(T):
        s = b - 4
        if s == 0:
            continue
        keep = (spot >= 4) & (spot < 4 + s) if s > 0 else (spot < 4) & (spot >= 4 + s)
        edge = edge + jnp.where(keep, roll(qbuf[b * KL : (b + 1) * KL, 0:LANES], s), 0.0)
    gbuf[...] = edge
    ends = (lane < 4) | (lane >= LANES - 4)
    bound = level[...]
    for i in range(8):
        qbuf[...] = jnp.dot(
            wa[:, 0 : T * wide], ebuf[i * wide : (i + T) * wide], preferred_element_type=F32
        )
        for half in range(2):
            row = i + 8 * half
            total = jnp.where(ends, roll(gbuf[...], -(8 * row + 4)), 0.0)
            for b in range(T):
                moved = roll(qbuf[b * KL : (b + 1) * KL, half * LANES : (half + 1) * LANES], b - 4)
                if b != 4:
                    moved = jnp.where(inside(lane, b - 4), moved, 0.0)
                total = total + moved
            shifted = codes[row] - (ETA_CODE * SCALE) * total
            codes[row] = shifted - jnp.clip(shifted, -bound, bound)


def correlation(err, codes, lbuf, cbuf, gacc, parts):
    lane = lane_index(C)
    rims = [gathered(err, 0), gathered(err, SLOTS - 1)]
    for row in range(EXT):
        main = gathered(err, row + 1)
        rim = roll(rims[row // 16], -(8 * (row % 16) + 4))
        for b in range(T):
            s = b - 4
            if s > 0:
                field = jnp.where(lane >= LANES - s, rim, main)
            elif s < 0:
                field = jnp.where(lane < -s, rim, main)
            else:
                field = main
            hi, lo = split(roll(field, s))
            at = row * 3 * LANES
            lbuf[b * C : (b + 1) * C, at : at + LANES] = hi
            lbuf[b * C : (b + 1) * C, at + LANES : at + 2 * LANES] = hi
            lbuf[b * C : (b + 1) * C, at + 2 * LANES : at + 3 * LANES] = lo
    none = jnp.zeros((KL, 3 * LANES), BF16)
    cbuf[0:KL, 0 : 3 * LANES] = none
    cbuf[ROWS * KL : (ROWS + 1) * KL, 3 * LANES : 6 * LANES] = none
    for i in range(ROWS):
        hi, lo = split(codes[i])
        for at, base in (((i + 1) * KL, 0), (i * KL, 3 * LANES)):
            cbuf[at : at + KL, base : base + LANES] = hi
            cbuf[at : at + KL, base + LANES : base + 2 * LANES] = lo
            cbuf[at : at + KL, base + 2 * LANES : base + 3 * LANES] = hi
    gacc[...] = jnp.zeros_like(gacc)
    for row in range(0, EXT, 2):
        low, high = max(row - 8, -1), min(row, ROWS - 1)
        a = low - row + 8
        count = (high - low + 1) * KL
        gacc[a * KL : a * KL + count] += lax.dot_general(
            cbuf[(low + 1) * KL : (low + 1) * KL + count],
            lbuf[:, row * 3 * LANES : (row + 2) * 3 * LANES],
            (((1,), (1,)), ((), ())),
            preferred_element_type=F32,
        )
    groups, share = parts.shape[1], parts.shape[3]
    for core in range(2):
        for g in range(groups):
            for a in range(T):
                at = a * KL + (2 * g + core) * share
                parts[core, g, a] = gacc[at : at + share]


def synthesis_weights(atoms, ws):
    for a in range(0, T + 1, 2):
        pairs = []
        for t in (a, a + 1):
            if t < T:
                field = jnp.concatenate([atoms[t, b] for b in range(T)], axis=0)
                hi, lo = split(field)
                pairs += [hi.astype(F32), hi.astype(F32), lo.astype(F32)]
            else:
                pairs += [jnp.zeros((T * C, KL), F32)] * 3
        for n in range(3):
            lanes = slice(a * 3 * KL + n * LANES, a * 3 * KL + (n + 1) * LANES)
            ws[:, lanes] = jnp.concatenate(pairs[2 * n : 2 * n + 2], axis=1).astype(BF16)


def adjoint_weights(atoms, flip, wa):
    depth = flip.shape[0]
    flip[T * 3 * C : depth] = jnp.zeros((depth - T * 3 * C, flip.shape[1]), F32)
    flip[:, T * KL :] = jnp.zeros((depth, flip.shape[1] - T * KL), F32)
    for a in range(T):
        at = (T - 1 - a) * 3 * C
        for b in range(0, T, 2):
            cols = slice(b * KL, min(b + 2, T) * KL)
            field = atoms[a, b]
            if b + 1 < T:
                field = jnp.concatenate([field, atoms[a, b + 1]], axis=1)
            hi, lo = split(field)
            flip[at : at + C, cols] = hi.astype(F32)
            flip[at + C : at + 2 * C, cols] = hi.astype(F32)
            flip[at + 2 * C : at + 3 * C, cols] = lo.astype(F32)
    for m in range(0, flip.shape[1], LANES):
        rows = min(LANES, T * KL - m)
        for n in range(0, depth, LANES):
            turned = jnp.transpose(flip[n : n + LANES, m : m + LANES])
            wa[m : m + rows, n : n + LANES] = turned[:rows].astype(BF16)


def owned_atoms(atoms, start, share, own):
    row = lax.broadcasted_iota(jnp.int32, (16, KL), 0)
    col = lax.broadcasted_iota(jnp.int32, (16, KL), 1)
    pick = jnp.where(col == row + start, 1.0, 0.0).astype(BF16)
    for a in range(T):
        field = jnp.concatenate([atoms[a, b] for b in range(T)], axis=0)
        hi, rest = field.astype(BF16), None
        rest = field - hi.astype(F32)
        mid = rest.astype(BF16)
        low = (rest - mid.astype(F32)).astype(BF16)
        total = None
        for piece in (hi, mid, low):
            part = lax.dot_general(
                pick, piece, (((1,), (1,)), ((), ())), preferred_element_type=F32
            )
            total = part if total is None else total + part
        own[a] = total[:share]


def greet(peers):
    barrier = pltpu.get_barrier_semaphore()
    for peer in peers:
        pl.semaphore_signal(barrier, inc=1, device_id=peer, device_id_type=MESH)


def greeted(peers):
    pl.semaphore_wait(pltpu.get_barrier_semaphore(), len(peers))


def send(src, dst, sems, slot, peer):
    copy = pltpu.make_async_remote_copy(
        src_ref=src,
        dst_ref=dst,
        send_sem=sems.at[0, slot],
        recv_sem=sems.at[1, slot],
        device_id=peer,
        device_id_type=MESH,
    )
    copy.start()
    return copy


def wait_all(copies):
    for copy in copies:
        copy.wait_recv()
    for copy in copies:
        copy.wait_send()


class Grid:
    def __init__(self, owners, rows, cols):
        self.owners, self.rows, self.cols, self.halves = owners, rows, cols, cols // 2
        self.q, self.r, self.c = (lax.axis_index(n) for n in ("atom", "row", "col"))
        q, r, c = self.q, self.r, self.c
        self.core, self.z = lax.rem(c, 2), lax.div(c, 2)
        self.peers = [{"atom": lax.rem(q + d, owners)} for d in range(1, owners)]
        self.up, self.down = {"row": lax.rem(r + rows - 1, rows)}, {"row": lax.rem(r + 1, rows)}
        self.left, self.right = {"col": lax.rem(c + cols - 1, cols)}, {"col": lax.rem(c + 1, cols)}
        self.partner = {"col": 2 * self.z + 1 - self.core}
        self.blocks = []
        for dr in range(rows):
            for dz in range(self.halves):
                if dr + dz > 0:
                    pr, pz = lax.rem(r + dr, rows), lax.rem(self.z + dz, self.halves)
                    place = {"row": pr, "col": 2 * pz + self.core}
                    self.blocks.append((pr * self.halves + pz, place))
        self.everyone = self.peers + [self.left, self.right] + [p for _, p in self.blocks]


def exchange(grid, part, image, err, rbuf, piece, piece2, h1, msg, h2, field, sems, meanwhile):
    s_rs, s_h1, s_h2, s_ag = sems
    owners, rows, cols, share = grid.owners, grid.rows, grid.cols, C // grid.owners
    copies = [send(part.at[p["atom"]], rbuf.at[d], s_rs, d, p) for d, p in enumerate(grid.peers)]
    meanwhile()
    wait_all(copies)
    total = part[grid.q]
    for d in range(owners - 1):
        total = total + rbuf[d]
    total = total * SCALE
    piece[0:5] = total[0:5]
    piece[5:21] = total[5:21] - image[...]
    piece[21:SLOTS] = total[21:SLOTS]

    f_up, f_down = (grid.r > 0).astype(F32), (grid.r < rows - 1).astype(F32)
    f_left, f_right = (grid.c > 0).astype(F32), (grid.c < cols - 1).astype(F32)
    lane = lane_index(share)
    wait_all(
        [
            send(piece.at[17:26], h1.at[0], s_h1, 0, grid.down),
            send(piece.at[0:9], h1.at[1], s_h1, 1, grid.up),
        ]
    )
    piece2[0] = piece[0] + h1[0, 8] * f_up
    piece2[1:9] = piece[1:9] + h1[0, 0:8] * f_up
    piece2[9:17] = piece[9:17]
    piece2[17:25] = piece[17:25] + h1[1, 1:9] * f_down
    piece2[25] = piece[25] + jnp.where(lane < 64, h1[1, 0], 0.0) * f_down

    ends = (lane < 4) | (lane >= LANES - 4)
    low = lane % 8 < 4
    packed = [jnp.zeros((share, LANES), F32), jnp.zeros((share, LANES), F32)]
    for row in range(EXT):
        packed[row // 16] += roll(jnp.where(ends, piece2[row + 1], 0.0), 8 * (row % 16) + 4)
    rims = [piece2[0], piece2[SLOTS - 1]]
    for v in range(2):
        msg[0, v] = jnp.where(low, packed[v], rims[v])
        msg[1, v] = jnp.where(low, rims[v], packed[v])
    wait_all(
        [
            send(msg.at[0], h2.at[0], s_h2, 0, grid.right),
            send(msg.at[1], h2.at[1], s_h2, 1, grid.left),
        ]
    )
    inner = [None, None]
    for v in range(2):
        from_left, from_right = h2[0, v] * f_left, h2[1, v] * f_right
        rims[v] = rims[v] + jnp.where(low, from_left, from_right)
        inner[v] = jnp.where(low, from_right, from_left)
        rims[v] = rims[v] * jnp.where(low, f_left, f_right)
    for row in range(EXT):
        fix = roll(inner[row // 16], -(8 * (row % 16) + 4))
        value = piece2[row + 1] + jnp.where(ends, fix, 0.0)
        if row < 4:
            value = value * f_up
        if row >= EXT - 4:
            value = value * f_down
        field[row + 1] = value
    field[0] = rims[0] * jnp.where(lane < 32, f_up, 1.0)
    field[SLOTS - 1] = jnp.where(lane < 64, rims[1] * jnp.where(lane >= 32, f_down, 1.0), 0.0)

    copies = [send(field, err.at[grid.q], s_ag, d, p) for d, p in enumerate(grid.peers)]
    err[grid.q] = field[...]
    wait_all(copies)


def update(grid, parts, own, velocity, new_atoms, new_velocity, half, total, chunks, s1, s2):
    wait_all([send(parts.at[1 - grid.core], half, s1, 0, grid.partner)])
    total[...] = parts[grid.core] + half[...]
    wait_all([send(total.at[g], chunks.at[d], s2, d, p) for d, (g, p) in enumerate(grid.blocks)])
    summed = total[grid.r * grid.halves + grid.z]
    for d in range(len(grid.blocks)):
        summed = summed + chunks[d]
    pixels = ROWS * LANES * grid.rows * grid.cols
    summed = summed * (1.0 / pixels)
    square = None
    for b in range(T):
        cols = slice(b * C, (b + 1) * C)
        fresh = MOMENTUM * velocity[:, b] + summed[:, :, cols]
        stepped = own[:, :, cols] - LEARN_RATE * fresh
        new_velocity[:, b] = fresh
        new_atoms[:, b] = stepped
        term = jnp.sum(stepped * stepped, axis=0)
        square = term if square is None else square + term
    square = jnp.sum(square, axis=1, keepdims=True) * (1.0 / (T * T * C))
    gain = lax.rsqrt(square + EPSILON)
    for b in range(T):
        new_atoms[:, b] = new_atoms[:, b] * gain[None]


def kernel(sizes, names, image, warm, atoms, limits, velocity, new_codes, new_atoms, new_velocity, *scratch):
    u = dict(zip(names, scratch))
    grid = Grid(*sizes)
    share, owned = C // grid.owners, velocity.shape[2]
    greet(grid.everyone)
    codes = u["codes"]
    loads = [pltpu.make_async_copy(atoms, u["atoms"], u["s_in"].at[0])]
    for i in range(ROWS):
        loads.append(pltpu.make_async_copy(warm.at[:, i], codes.at[i], u["s_in"].at[1 + i]))
    for i in range(ROWS):
        bands = image.at[pl.ds(grid.q * share, share), i]
        loads.append(pltpu.make_async_copy(bands, u["image"].at[i], u["s_in"].at[1 + ROWS + i]))
    for load in loads:
        load.start()
    diagonal = lax.broadcasted_iota(jnp.int32, (KL, KL), 0) == lax.broadcasted_iota(
        jnp.int32, (KL, KL), 1
    )
    column = jnp.sum(jnp.where(diagonal, limits[...], 0.0), axis=1, keepdims=True)
    u["level"][...] = jnp.broadcast_to(ETA_CODE * column, (KL, LANES))
    loads[0].wait()
    synthesis_weights(u["atoms"], u["ws"])
    for load in loads[1:]:
        load.wait()
    synthesis(codes, u["ws"], u["zbuf"], u["acc"], u["part"])

    def meet(n, meanwhile):
        exchange(
            grid,
            u["part"],
            u["image"],
            u["err"].at[n],
            u["rbuf"].at[n],
            u["piece"],
            u["piece2"],
            u["h1"].at[n],
            u["msg"],
            u["h2"].at[n],
            u["field"],
            [u[s].at[n] for s in ("s_rs", "s_h1", "s_h2", "s_ag")],
            meanwhile,
        )

    def prepare():
        adjoint_weights(u["atoms"], u["flip"], u["wa"])
        start = (grid.r * grid.cols + grid.c) * owned
        owned_atoms(u["atoms"], start, owned, u["own"])

    greeted(grid.everyone)
    meet(0, prepare)

    def one(n, carry):
        buffers = [u[s] for s in ("ebuf", "hbuf", "qbuf", "gbuf")]
        adjoint_step(u["err"].at[n - 1], u["wa"], u["level"], codes, *buffers)
        synthesis(codes, u["ws"], u["zbuf"], u["acc"], u["part"])
        meet(n, lambda: None)
        return carry

    lax.fori_loop(1, ITERS + 1, one, 0)
    stores = [
        pltpu.make_async_copy(codes.at[i], new_codes.at[:, i], u["s_in"].at[i]) for i in range(ROWS)
    ]
    for store in stores:
        store.start()
    correlation(u["err"].at[ITERS], codes, u["lbuf"], u["cbuf"], u["gacc"], u["parts"])
    buffers = [u[s] for s in ("half", "total", "chunks", "s_core", "s_block")]
    update(grid, u["parts"], u["own"], velocity, new_atoms, new_velocity, *buffers)
    for store in stores:
        store.wait()


def struct(shape, dtype=F32):
    return jax.ShapeDtypeStruct(shape, dtype)


def shards(hyper_image, warm_codes, dictionary, thresholds, velocity):
    owners, rows, cols = lax.axis_size("atom"), lax.axis_size("row"), lax.axis_size("col")
    share, owned, halves = C // owners, velocity.shape[0], cols // 2
    rounds, groups = ITERS + 1, rows * halves
    piece = pltpu.VMEM((SLOTS, share, LANES), F32)
    chunk = (T, owned, T * C)
    sems = pltpu.SemaphoreType.DMA
    scratch = {
        "codes": pltpu.VMEM((ROWS, KL, LANES), F32),
        "atoms": pltpu.VMEM((T, T, C, KL), F32),
        "image": pltpu.VMEM((ROWS, share, LANES), F32),
        "level": pltpu.VMEM((KL, LANES), F32),
        "ws": pltpu.VMEM((T * C, (T + 1) * 3 * KL), BF16),
        "flip": pltpu.VMEM((7 * LANES, 5 * LANES), F32),
        "wa": pltpu.VMEM((T * KL, 7 * LANES), BF16),
        "own": pltpu.VMEM(chunk, F32),
        "zbuf": pltpu.VMEM((10 * 3 * KL, 2 * LANES), BF16),
        "acc": pltpu.VMEM((8, C, LANES), F32),
        "part": pltpu.VMEM((owners, SLOTS, share, LANES), F32),
        "err": pltpu.VMEM((rounds, owners, SLOTS, share, LANES), F32),
        "rbuf": pltpu.VMEM((rounds, owners - 1, SLOTS, share, LANES), F32),
        "piece": piece,
        "piece2": piece,
        "h1": pltpu.VMEM((rounds, 2, 9, share, LANES), F32),
        "msg": pltpu.VMEM((2, 2, share, LANES), F32),
        "h2": pltpu.VMEM((rounds, 2, 2, share, LANES), F32),
        "field": piece,
        "ebuf": pltpu.VMEM((16 * 3 * C, 2 * LANES), BF16),
        "hbuf": pltpu.VMEM((T * 3 * C, LANES), BF16),
        "qbuf": pltpu.VMEM((T * KL, 2 * LANES), F32),
        "gbuf": pltpu.VMEM((KL, LANES), F32),
        "lbuf": pltpu.VMEM((T * C, EXT * 3 * LANES), BF16),
        "cbuf": pltpu.VMEM(((ROWS + 1) * KL, 6 * LANES), BF16),
        "gacc": pltpu.VMEM((T * KL, T * C), F32),
        "parts": pltpu.VMEM((2, groups) + chunk, F32),
        "half": pltpu.VMEM((groups,) + chunk, F32),
        "total": pltpu.VMEM((groups,) + chunk, F32),
        "chunks": pltpu.VMEM((groups - 1,) + chunk, F32),
        "s_in": sems((1 + 2 * ROWS,)),
        "s_rs": sems((rounds, 2, owners - 1)),
        "s_h1": sems((rounds, 2, 2)),
        "s_h2": sems((rounds, 2, 2)),
        "s_ag": sems((rounds, 2, owners - 1)),
        "s_core": sems((2, 1)),
        "s_block": sems((2, groups - 1)),
    }
    natural = (T, T, owned, C)
    new_codes, new_atoms, new_velocity = pl.pallas_call(
        functools.partial(kernel, (owners, rows, cols), tuple(scratch)),
        out_shape=(struct((KL, ROWS, LANES)), struct(natural), struct(natural)),
        in_specs=[ANY, ANY, ANY, VMEM, VMEM],
        out_specs=(ANY, VMEM, VMEM),
        scratch_shapes=list(scratch.values()),
        compiler_params=pltpu.CompilerParams(
            vmem_limit_bytes=60 << 20, collective_id=0, has_side_effects=True
        ),
    )(
        hyper_image,
        warm_codes,
        dictionary.transpose(1, 2, 3, 0),
        thresholds.reshape(1, KL),
        velocity.transpose(1, 2, 0, 3),
    )
    return new_codes, new_atoms.transpose(2, 0, 1, 3), new_velocity.transpose(2, 0, 1, 3)


def solution(mesh):
    in_specs = (
        P(None, "row", "col"),
        P("atom", "row", "col"),
        P("atom", None, None, None),
        P("atom"),
        P(("atom", "row", "col"), None, None, None),
    )
    out_specs = (
        P("atom", "row", "col"),
        P(("atom", "row", "col"), None, None, None),
        P(("atom", "row", "col"), None, None, None),
    )
    return jax.shard_map(shards, mesh=mesh, in_specs=in_specs, out_specs=out_specs, check_vma=False)
```

```python
import functools
import math

import jax
import jax.numpy as jnp
from jax import lax
from jax.experimental import pallas as pl
from jax.experimental.pallas import tpu as pltpu
from jax.sharding import PartitionSpec as P

ITERS = 2
ETA_CODE = 0.05
MOMENTUM = 0.9
LEARN_RATE = 200.0
EPSILON = 1e-06

F32 = jnp.float32
BF16 = jnp.bfloat16
MESH = pl.DeviceIdType.MESH
VMEM = pl.BlockSpec(memory_space=pltpu.VMEM)
ANY = pl.BlockSpec(memory_space=pl.ANY)

C = 32
T = 9
KL = 64
ROWS = 16
LANES = 128
EXT = ROWS + 8
SLOTS = EXT + 2
SCALE = 1.0 / math.sqrt(T * T * C)
READY = ((0, 8), (8, 16), (16, 26))
RUNS = (
    ((0, 4, 0), (4, 8, 4)),
    ((8, 12, 8), (12, 16, 16)),
    ((16, 20, 12), (20, 24, 20), (24, 25, -1), (25, 26, -2)),
)
PLACE = [0] * EXT
for _runs in RUNS:
    for _low, _high, _row in _runs:
        for _n in range(_high - _low):
            if _row >= 0:
                PLACE[_row + _n] = _low + _n
PARTS = ((0, 10), (10, 18), (18, 26))
GROUP = 3


def split(x):
    hi = x.astype(BF16)
    return hi, (x - hi.astype(F32)).astype(BF16)


def lane_index(rows):
    return lax.broadcasted_iota(jnp.int32, (rows, LANES), 1)


def roll(x, shift):
    return pltpu.roll(x, shift % LANES, 1) if shift % LANES else x


def inside(lane, shift):
    return lane >= shift if shift > 0 else lane < LANES + shift


def synthesis(codes, ws, zbuf, acc, part, ready):
    owners = part.shape[0]
    share = C // owners
    lane = lane_index(C)
    zero_rows = jnp.zeros((3 * KL, 2 * LANES), BF16)
    zbuf[0 : 3 * KL] = zero_rows
    zbuf[9 * 3 * KL : 10 * 3 * KL] = zero_rows
    for t in range(8):
        hi, lo = split(jnp.concatenate([codes[t], codes[t + 8]], axis=1))
        base = (t + 1) * 3 * KL
        zbuf[base : base + KL] = hi
        zbuf[base + KL : base + 2 * KL] = lo
        zbuf[base + 2 * KL : base + 3 * KL] = hi
    rims = [jnp.zeros((C, LANES), F32), jnp.zeros((C, LANES), F32)]

    def put(slot, row):
        for q in range(owners):
            part[q, slot] = row[q * share : (q + 1) * share]

    for ho in range(16):
        first, last = max(0, 8 - ho) // 2, min(8, 15 - ho) // 2
        depth = (last - first + 1) * 6 * KL
        start = (2 * first + ho - 7) * 3 * KL
        taps = jnp.dot(
            ws[:, first * 6 * KL : first * 6 * KL + depth],
            zbuf[start : start + depth],
            preferred_element_type=F32,
        )
        for half in range(2):
            main = jnp.zeros((C, LANES), F32)
            rim = jnp.zeros((C, LANES), F32)
            for b in range(T):
                moved = roll(taps[b * C : (b + 1) * C, half * LANES : (half + 1) * LANES], 4 - b)
                if b == 4:
                    main = main + moved
                else:
                    keep = inside(lane, 4 - b)
                    main = main + jnp.where(keep, moved, 0.0)
                    rim = rim + jnp.where(keep, 0.0, moved)
            row = ho + 8 * half
            rims[row // 16] = rims[row // 16] + roll(rim, 8 * (row % 16) + 4)
            if half == 0 and ho >= 8:
                main = main + acc[ho - 8]
            if half == 1 and ho < 8:
                acc[ho] = main
            else:
                put(PLACE[row], main)
        if ho in (7, 11):
            ready(ho // 4 - 1)
    put(24, rims[0])
    put(25, rims[1])
    ready(2)


def gathered(err, slot):
    return jnp.concatenate([err[q, slot] for q in range(err.shape[0])], axis=0)


def adjoint_step(err, arrived, wa, level, codes, ebuf, hbuf, qbuf, gbuf):
    wide = 3 * C
    lane_c = lane_index(C)
    lane = lane_index(KL)
    spot = lane % 8
    arrived(0)
    rims = [gathered(err, 0), gathered(err, 1)]
    for t in range(T):
        hi, lo = split(
            jnp.where(lane_c < LANES - 8 * t, roll(rims[0], -8 * t), roll(rims[1], -8 * t))
        )
        hbuf[t * wide : t * wide + C] = hi
        hbuf[t * wide + C : t * wide + 2 * C] = lo
        hbuf[t * wide + 2 * C : t * wide + 3 * C] = hi
    qbuf[:, 0:LANES] = jnp.dot(wa[:, 0 : T * wide], hbuf[...], preferred_element_type=F32)
    edge = jnp.zeros((KL, LANES), F32)
    for b in range(T):
        s = b - 4
        if s == 0:
            continue
        keep = (spot >= 4) & (spot < 4 + s) if s > 0 else (spot < 4) & (spot >= 4 + s)
        edge = edge + jnp.where(keep, roll(qbuf[b * KL : (b + 1) * KL, 0:LANES], s), 0.0)
    gbuf[...] = edge
    for row in range(EXT):
        if row in (8, 16):
            arrived(row // 8)
        hi, lo = split(gathered(err, row + 2))
        for t, side in ((row, 0), (row - 8, 1)):
            if 0 <= t < 16:
                cols = slice(side * LANES, (side + 1) * LANES)
                ebuf[t * wide : t * wide + C, cols] = hi
                ebuf[t * wide + C : t * wide + 2 * C, cols] = lo
                ebuf[t * wide + 2 * C : t * wide + 3 * C, cols] = hi
    ends = (lane < 4) | (lane >= LANES - 4)
    bound = level[...]
    for i in range(8):
        qbuf[...] = jnp.dot(
            wa[:, 0 : T * wide], ebuf[i * wide : (i + T) * wide], preferred_element_type=F32
        )
        for half in range(2):
            row = i + 8 * half
            total = jnp.where(ends, roll(gbuf[...], -(8 * row + 4)), 0.0)
            for b in range(T):
                moved = roll(qbuf[b * KL : (b + 1) * KL, half * LANES : (half + 1) * LANES], b - 4)
                if b != 4:
                    moved = jnp.where(inside(lane, b - 4), moved, 0.0)
                total = total + moved
            shifted = codes[row] - (ETA_CODE * SCALE) * total
            codes[row] = shifted - jnp.clip(shifted, -bound, bound)


def stacked_codes(codes, cbuf):
    wide = 3 * LANES
    none = jnp.zeros((KL, wide), BF16)
    for i in range(-2, ROWS + 2):
        inner = 0 <= i < ROWS
        if inner:
            hi, lo = split(codes[i])
        for n in range(GROUP):
            u = i + 2 - n
            if not 0 <= u < ROWS + 2:
                continue
            rows = slice(n * KL, (n + 1) * KL)
            if inner:
                cbuf[rows, u * wide : u * wide + LANES] = hi
                cbuf[rows, u * wide + LANES : u * wide + 2 * LANES] = lo
                cbuf[rows, u * wide + 2 * LANES : u * wide + 3 * LANES] = hi
            else:
                cbuf[rows, u * wide : (u + 1) * wide] = none


def shifted_errors(err, arrived, lbuf):
    lane = lane_index(C)
    arrived(0)
    rims = [gathered(err, 0), gathered(err, 1)]
    for row in range(EXT):
        if row in (8, 16):
            arrived(row // 8)
        main = gathered(err, row + 2)
        rim = roll(rims[row // 16], -(8 * (row % 16) + 4))
        for b in range(T):
            s = b - 4
            if s > 0:
                field = jnp.where(lane >= LANES - s, rim, main)
            elif s < 0:
                field = jnp.where(lane < -s, rim, main)
            else:
                field = main
            hi, lo = split(roll(field, s))
            at = row * 3 * LANES
            lbuf[b * C : (b + 1) * C, at : at + LANES] = hi
            lbuf[b * C : (b + 1) * C, at + LANES : at + 2 * LANES] = hi
            lbuf[b * C : (b + 1) * C, at + 2 * LANES : at + 3 * LANES] = lo


def correlation(group, lbuf, cbuf, gacc, parts):
    first, depth = group * GROUP, (ROWS + 2) * 3 * LANES
    start = (6 - first) * 3 * LANES
    gacc[0 : T * C, 0 : GROUP * KL] = lax.dot_general(
        lbuf[:, start : start + depth],
        cbuf[...],
        (((1,), (1,)), ((), ())),
        preferred_element_type=F32,
    )
    groups, share = parts.shape[1], parts.shape[3]
    for m in range(0, 2 * LANES, LANES):
        for n in range(0, 3 * LANES, LANES):
            turned = jnp.transpose(gacc[n : n + LANES, m : m + LANES])
            width = min(LANES, T * C - n)
            for k in range(0, min(LANES, GROUP * KL - m), share):
                a, block = first + (m + k) // KL, (k % KL) // share
                parts[block % 2, block // 2, a, :, n : n + width] = turned[k : k + share, :width]


def synthesis_weights(atoms, ws):
    for a in range(0, T + 1, 2):
        pairs = []
        for t in (a, a + 1):
            if t < T:
                field = jnp.concatenate([atoms[t, b] for b in range(T)], axis=0)
                hi, lo = split(field)
                pairs += [hi.astype(F32), hi.astype(F32), lo.astype(F32)]
            else:
                pairs += [jnp.zeros((T * C, KL), F32)] * 3
        for n in range(3):
            lanes = slice(a * 3 * KL + n * LANES, a * 3 * KL + (n + 1) * LANES)
            ws[:, lanes] = jnp.concatenate(pairs[2 * n : 2 * n + 2], axis=1).astype(BF16)


def adjoint_weights(atoms, flip, wa):
    depth = flip.shape[0]
    flip[T * 3 * C : depth] = jnp.zeros((depth - T * 3 * C, flip.shape[1]), F32)
    flip[:, T * KL :] = jnp.zeros((depth, flip.shape[1] - T * KL), F32)
    for a in range(T):
        at = (T - 1 - a) * 3 * C
        for b in range(0, T, 2):
            cols = slice(b * KL, min(b + 2, T) * KL)
            field = atoms[a, b]
            if b + 1 < T:
                field = jnp.concatenate([field, atoms[a, b + 1]], axis=1)
            hi, lo = split(field)
            flip[at : at + C, cols] = hi.astype(F32)
            flip[at + C : at + 2 * C, cols] = hi.astype(F32)
            flip[at + 2 * C : at + 3 * C, cols] = lo.astype(F32)
    for m in range(0, flip.shape[1], LANES):
        rows = min(LANES, T * KL - m)
        for n in range(0, depth, LANES):
            turned = jnp.transpose(flip[n : n + LANES, m : m + LANES])
            wa[m : m + rows, n : n + LANES] = turned[:rows].astype(BF16)


def owned_atoms(atoms, start, share, own):
    row = lax.broadcasted_iota(jnp.int32, (16, KL), 0)
    col = lax.broadcasted_iota(jnp.int32, (16, KL), 1)
    pick = jnp.where(col == row + start, 1.0, 0.0).astype(BF16)
    for a in range(T):
        field = jnp.concatenate([atoms[a, b] for b in range(T)], axis=0)
        hi, rest = field.astype(BF16), None
        rest = field - hi.astype(F32)
        mid = rest.astype(BF16)
        low = (rest - mid.astype(F32)).astype(BF16)
        total = None
        for piece in (hi, mid, low):
            part = lax.dot_general(
                pick, piece, (((1,), (1,)), ((), ())), preferred_element_type=F32
            )
            total = part if total is None else total + part
        own[a] = total[:share]


def greet(peers):
    barrier = pltpu.get_barrier_semaphore()
    for peer in peers:
        pl.semaphore_signal(barrier, inc=1, device_id=peer, device_id_type=MESH)


def greeted(peers):
    pl.semaphore_wait(pltpu.get_barrier_semaphore(), len(peers))


def send(src, dst, sems, slot, peer):
    copy = remote(src, dst, sems, slot, peer)
    copy.start()
    return copy


class Grid:
    def __init__(self, owners, rows, cols):
        self.owners, self.rows, self.cols, self.halves = owners, rows, cols, cols // 2
        self.q, self.r, self.c = (lax.axis_index(n) for n in ("atom", "row", "col"))
        q, r, c = self.q, self.r, self.c
        self.core, self.z = lax.rem(c, 2), lax.div(c, 2)
        self.peers = [{"atom": lax.rem(q + d, owners)} for d in range(1, owners)]
        self.up, self.down = {"row": lax.rem(r + rows - 1, rows)}, {"row": lax.rem(r + 1, rows)}
        self.left, self.right = {"col": lax.rem(c + cols - 1, cols)}, {"col": lax.rem(c + 1, cols)}
        self.partner = {"col": 2 * self.z + 1 - self.core}
        self.blocks = []
        for dr in range(rows):
            for dz in range(self.halves):
                if dr + dz > 0:
                    pr, pz = lax.rem(r + dr, rows), lax.rem(self.z + dz, self.halves)
                    place = {"row": pr, "col": 2 * pz + self.core}
                    self.blocks.append((pr * self.halves + pz, place))
        self.corners = [{**v, **h} for v in (self.up, self.down) for h in (self.left, self.right)]
        self.everyone = self.peers + [self.left, self.right] + [p for _, p in self.blocks]
        self.everyone += self.corners


def remote(src, dst, sems, slot, peer):
    return pltpu.make_async_remote_copy(
        src_ref=src,
        dst_ref=dst,
        send_sem=sems.at[0, slot],
        recv_sem=sems.at[1, slot],
        device_id=peer,
        device_id_type=MESH,
    )


def sum_copies(grid, u, n, chunk):
    low, high = READY[chunk]
    count = grid.owners - 1
    return [
        remote(
            u["part"].at[p["atom"], low:high],
            u["rbuf"].at[n, d, low:high],
            u["s_rs"].at[n],
            chunk * count + d,
            p,
        )
        for d, p in enumerate(grid.peers)
    ]


def meet(grid, u, n):
    share, rows, cols = C // grid.owners, grid.rows, grid.cols
    piece, field, image = u["piece"], u["field"], u["image"]
    h1, h2, h3, msg, err = u["h1"].at[n], u["h2"].at[n], u["h3"].at[n], u["msg"], u["err"].at[n]
    part, rbuf = u["part"], u["rbuf"].at[n]
    for chunk, runs in enumerate(RUNS):
        for copy in sum_copies(grid, u, n, chunk):
            copy.wait_recv()
        for low, high, row in runs:
            total = part[grid.q, low:high]
            for d in range(grid.owners - 1):
                total = total + rbuf[d, low:high]
            total = total * SCALE
            if 4 <= row < 4 + ROWS:
                total = total - image[row - 4 : row - 4 + high - low]
            at = row + 1 if row >= 0 else (0 if row == -1 else SLOTS - 1)
            piece[at : at + high - low] = total

    edges = [
        send(piece.at[17:26], h1.at[0], u["s_h1"].at[n], 0, grid.down),
        send(piece.at[0:9], h1.at[1], u["s_h1"].at[n], 1, grid.up),
    ]
    f_up, f_down = (grid.r > 0).astype(F32), (grid.r < rows - 1).astype(F32)
    f_left, f_right = (grid.c > 0).astype(F32), (grid.c < cols - 1).astype(F32)
    lane = lane_index(share)
    ends = (lane < 4) | (lane >= LANES - 4)
    low = lane % 8 < 4
    packed = [jnp.zeros((share, LANES), F32), jnp.zeros((share, LANES), F32)]
    for row in range(EXT):
        packed[row // 16] += roll(jnp.where(ends, piece[row + 1], 0.0), 8 * (row % 16) + 4)
    own = [piece[0], piece[SLOTS - 1]]
    for v in range(2):
        msg[0, v] = jnp.where(low, packed[v], own[v])
        msg[1, v] = jnp.where(low, own[v], packed[v])
    edges += [
        send(msg.at[0, 1], h3.at[0], u["s_h3"].at[n], 0, grid.corners[3]),
        send(msg.at[0, 0], h3.at[1], u["s_h3"].at[n], 1, grid.corners[1]),
        send(msg.at[1, 1], h3.at[2], u["s_h3"].at[n], 2, grid.corners[2]),
        send(msg.at[1, 0], h3.at[3], u["s_h3"].at[n], 3, grid.corners[0]),
        send(msg.at[0], h2.at[0], u["s_h2"].at[n], 0, grid.right),
        send(msg.at[1], h2.at[1], u["s_h2"].at[n], 1, grid.left),
    ]
    for copy in edges:
        copy.wait_recv()
    begin = lane < 64
    sides = []
    for side, factor in ((0, f_left), (1, f_right)):
        above = h3[2 * side] * f_up
        below = jnp.where(begin, h3[2 * side + 1], 0.0) * f_down
        sides.append([(h2[side, 0] + above) * factor, (h2[side, 1] + below) * factor])
    rims = [own[0] + h1[0, 8] * f_up, own[1] + jnp.where(begin, h1[1, 0], 0.0) * f_down]
    inner = [None, None]
    for v in range(2):
        from_left, from_right = sides[0][v], sides[1][v]
        rims[v] = rims[v] + jnp.where(low, from_left, from_right)
        inner[v] = jnp.where(low, from_right, from_left)
        rims[v] = rims[v] * jnp.where(low, f_left, f_right)
    field[0] = rims[0] * jnp.where(lane < 32, f_up, 1.0)
    field[1] = jnp.where(begin, rims[1] * jnp.where(lane >= 32, f_down, 1.0), 0.0)
    copies = []
    for row in range(EXT):
        fix = roll(inner[row // 16], -(8 * (row % 16) + 4))
        value = piece[row + 1]
        if row < 8:
            value = value + h1[0, row] * f_up
        if row >= 16:
            value = value + h1[1, row - 15] * f_down
        value = value + jnp.where(ends, fix, 0.0)
        if row < 4:
            value = value * f_up
        if row >= EXT - 4:
            value = value * f_down
        field[row + 2] = value
        if row % 8 == 7:
            chunk = row // 8
            first, last = PARTS[chunk]
            copies.append(
                [
                    send(
                        field.at[first:last],
                        err.at[grid.q, first:last],
                        u["s_ag"].at[n],
                        chunk * (grid.owners - 1) + d,
                        p,
                    )
                    for d, p in enumerate(grid.peers)
                ]
            )
            err[grid.q, first:last] = field[first:last]
    for chunk in range(len(READY)):
        for copy in sum_copies(grid, u, n, chunk):
            copy.wait_send()
    for copy in edges:
        copy.wait_send()

    def arrived(chunk):
        for copy in copies[chunk]:
            copy.wait_recv()
        if chunk == 2:
            for group in copies:
                for copy in group:
                    copy.wait_send()

    return arrived


def kernel(sizes, names, owned, image, warm, atoms, limits, new_codes, grad, picked, *scratch):
    u = dict(zip(names, scratch))
    grid = Grid(*sizes)
    share = C // grid.owners
    greet(grid.everyone)
    codes = u["codes"]
    loads = [pltpu.make_async_copy(atoms, u["atoms"], u["s_in"].at[0])]
    for i in range(ROWS):
        loads.append(pltpu.make_async_copy(warm.at[:, i], codes.at[i], u["s_in"].at[1 + i]))
    for i in range(ROWS):
        bands = image.at[pl.ds(grid.q * share, share), i]
        loads.append(pltpu.make_async_copy(bands, u["image"].at[i], u["s_in"].at[1 + ROWS + i]))
    for load in loads:
        load.start()
    diagonal = lax.broadcasted_iota(jnp.int32, (KL, KL), 0) == lax.broadcasted_iota(
        jnp.int32, (KL, KL), 1
    )
    column = jnp.sum(jnp.where(diagonal, limits[...], 0.0), axis=1, keepdims=True)
    u["level"][...] = jnp.broadcast_to(ETA_CODE * column, (KL, LANES))
    loads[0].wait()
    synthesis_weights(u["atoms"], u["ws"])
    for load in loads[1:]:
        load.wait()

    def partial_sums(n, begin):
        def ready(chunk):
            if chunk == 0:
                begin()
            for copy in sum_copies(grid, u, n, chunk):
                copy.start()

        synthesis(codes, u["ws"], u["zbuf"], u["acc"], u["part"], ready)

    partial_sums(0, lambda: greeted(grid.everyone))
    adjoint_weights(u["atoms"], u["flip"], u["wa"])
    owned_atoms(u["atoms"], (grid.r * grid.cols + grid.c) * owned, owned, picked)

    def one(n, carry):
        arrived = meet(grid, u, n)
        buffers = [u[s] for s in ("ebuf", "hbuf", "qbuf", "gbuf")]
        adjoint_step(u["err"].at[n], arrived, u["wa"], u["level"], codes, *buffers)
        partial_sums(n + 1, lambda: None)
        return carry

    lax.fori_loop(0, ITERS, one, 0)
    stores = [
        pltpu.make_async_copy(codes.at[i], new_codes.at[:, i], u["s_in"].at[i]) for i in range(ROWS)
    ]
    for store in stores:
        store.start()
    stacked_codes(codes, u["cbuf"])
    arrived = meet(grid, u, ITERS)
    shifted_errors(u["err"].at[ITERS], arrived, u["lbuf"])

    parts, half, total, chunks = (u[s] for s in ("parts", "half", "total", "chunks"))
    pairs, blocks = [], []

    def taps(group):
        return slice(group * GROUP, (group + 1) * GROUP)

    def spread(group):
        pairs[group].wait_recv()
        at = taps(group)
        total[:, at] = parts[grid.core, :, at] + half[:, at]
        for d, (g, p) in enumerate(grid.blocks):
            slot = group * len(grid.blocks) + d
            blocks.append(send(total.at[g, at], chunks.at[d, at], u["s_block"], slot, p))

    for group in range(T // GROUP):
        correlation(group, u["lbuf"], u["cbuf"], u["gacc"], parts)
        at = taps(group)
        pairs.append(
            send(parts.at[1 - grid.core, :, at], half.at[:, at], u["s_core"], group, grid.partner)
        )
        if group > 0:
            spread(group - 1)
    spread(T // GROUP - 1)
    pixels = ROWS * LANES * grid.rows * grid.cols
    for group in range(T // GROUP):
        at = taps(group)
        for copy in blocks[group * len(grid.blocks) : (group + 1) * len(grid.blocks)]:
            copy.wait_recv()
        summed = total[grid.r * grid.halves + grid.z, at]
        for d in range(len(grid.blocks)):
            summed = summed + chunks[d, at]
        grad[at] = summed * (1.0 / pixels)
    for copy in pairs + blocks:
        copy.wait_send()
    for store in stores:
        store.wait()


def finish(codes, grad, own, velocity, new_codes, new_atoms, new_velocity, buffer, sems):
    read = pltpu.make_async_copy(codes, buffer, sems.at[0])
    read.start()
    square = None
    for b in range(T):
        cols = slice(b * C, (b + 1) * C)
        fresh = MOMENTUM * velocity[:, b] + grad[:, :, cols]
        stepped = own[:, :, cols] - LEARN_RATE * fresh
        new_velocity[:, b] = fresh
        new_atoms[:, b] = stepped
        term = jnp.sum(stepped * stepped, axis=0)
        square = term if square is None else square + term
    read.wait()
    write = pltpu.make_async_copy(buffer, new_codes, sems.at[1])
    write.start()
    square = jnp.sum(square, axis=1, keepdims=True) * (1.0 / (T * T * C))
    gain = lax.rsqrt(square + EPSILON)
    for b in range(T):
        new_atoms[:, b] = new_atoms[:, b] * gain[None]
    write.wait()


def struct(shape, dtype=F32):
    return jax.ShapeDtypeStruct(shape, dtype)


def shards(hyper_image, warm_codes, dictionary, thresholds, velocity):
    owners, rows, cols = lax.axis_size("atom"), lax.axis_size("row"), lax.axis_size("col")
    share, owned, halves = C // owners, velocity.shape[0], cols // 2
    rounds, groups = ITERS + 1, rows * halves
    piece = pltpu.VMEM((SLOTS, share, LANES), F32)
    chunk = (T, owned, T * C)
    sems = pltpu.SemaphoreType.DMA
    scratch = {
        "codes": pltpu.VMEM((ROWS, KL, LANES), F32),
        "atoms": pltpu.VMEM((T, T, C, KL), F32),
        "image": pltpu.VMEM((ROWS, share, LANES), F32),
        "level": pltpu.VMEM((KL, LANES), F32),
        "ws": pltpu.VMEM((T * C, (T + 1) * 3 * KL), BF16),
        "flip": pltpu.VMEM((7 * LANES, 5 * LANES), F32),
        "wa": pltpu.VMEM((T * KL, 7 * LANES), BF16),
        "zbuf": pltpu.VMEM((10 * 3 * KL, 2 * LANES), BF16),
        "acc": pltpu.VMEM((8, C, LANES), F32),
        "part": pltpu.VMEM((owners, SLOTS, share, LANES), F32),
        "err": pltpu.VMEM((rounds, owners, SLOTS, share, LANES), F32),
        "rbuf": pltpu.VMEM((rounds, owners - 1, SLOTS, share, LANES), F32),
        "piece": piece,
        "h1": pltpu.VMEM((rounds, 2, 9, share, LANES), F32),
        "msg": pltpu.VMEM((2, 2, share, LANES), F32),
        "h2": pltpu.VMEM((rounds, 2, 2, share, LANES), F32),
        "h3": pltpu.VMEM((rounds, 4, share, LANES), F32),
        "field": piece,
        "ebuf": pltpu.VMEM((16 * 3 * C, 2 * LANES), BF16),
        "hbuf": pltpu.VMEM((T * 3 * C, LANES), BF16),
        "qbuf": pltpu.VMEM((T * KL, 2 * LANES), F32),
        "gbuf": pltpu.VMEM((KL, LANES), F32),
        "lbuf": pltpu.VMEM((T * C, EXT * 3 * LANES), BF16),
        "cbuf": pltpu.VMEM((GROUP * KL, (ROWS + 2) * 3 * LANES), BF16),
        "gacc": pltpu.VMEM((3 * LANES, 2 * LANES), F32),
        "parts": pltpu.VMEM((2, groups) + chunk, F32),
        "half": pltpu.VMEM((groups,) + chunk, F32),
        "total": pltpu.VMEM((groups,) + chunk, F32),
        "chunks": pltpu.VMEM((groups - 1,) + chunk, F32),
        "s_in": sems((1 + 2 * ROWS,)),
        "s_rs": sems((rounds, 2, 3 * (owners - 1))),
        "s_h1": sems((rounds, 2, 2)),
        "s_h2": sems((rounds, 2, 2)),
        "s_h3": sems((rounds, 2, 4)),
        "s_ag": sems((rounds, 2, 3 * (owners - 1))),
        "s_core": sems((2, T // GROUP)),
        "s_block": sems((2, T // GROUP * (groups - 1))),
    }
    natural = (T, T, owned, C)
    codes, grad, own = pl.pallas_call(
        functools.partial(kernel, (owners, rows, cols), tuple(scratch), owned),
        out_shape=(struct((KL, ROWS, LANES)), struct(chunk), struct(chunk)),
        in_specs=[ANY, ANY, ANY, VMEM],
        out_specs=(ANY, VMEM, VMEM),
        scratch_shapes=list(scratch.values()),
        compiler_params=pltpu.CompilerParams(
            vmem_limit_bytes=60 << 20, collective_id=0, has_side_effects=True
        ),
    )(hyper_image, warm_codes, dictionary.transpose(1, 2, 3, 0), thresholds.reshape(1, KL))
    new_codes, new_atoms, new_velocity = pl.pallas_call(
        finish,
        out_shape=(struct((KL, ROWS, LANES)), struct(natural), struct(natural)),
        in_specs=[ANY, VMEM, VMEM, VMEM],
        out_specs=(ANY, VMEM, VMEM),
        scratch_shapes=[pltpu.VMEM((KL, ROWS, LANES), F32), sems((2,))],
    )(codes, grad, own, velocity.transpose(1, 2, 0, 3))
    return new_codes, new_atoms.transpose(2, 0, 1, 3), new_velocity.transpose(2, 0, 1, 3)


def solution(mesh):
    in_specs = (
        P(None, "row", "col"),
        P("atom", "row", "col"),
        P("atom", None, None, None),
        P("atom"),
        P(("atom", "row", "col"), None, None, None),
    )
    out_specs = (
        P("atom", "row", "col"),
        P(("atom", "row", "col"), None, None, None),
        P(("atom", "row", "col"), None, None, None),
    )
    return jax.shard_map(shards, mesh=mesh, in_specs=in_specs, out_specs=out_specs, check_vma=False)
```

```python
import functools
import math

import jax
import jax.numpy as jnp
from jax import lax
from jax.experimental import pallas as pl
from jax.experimental.pallas import tpu as pltpu
from jax.sharding import PartitionSpec as P

ITERS = 2
ETA_CODE = 0.05
MOMENTUM = 0.9
LEARN_RATE = 200.0
EPSILON = 1e-06

F32 = jnp.float32
BF16 = jnp.bfloat16
MESH = pl.DeviceIdType.MESH
VMEM = pl.BlockSpec(memory_space=pltpu.VMEM)
ANY = pl.BlockSpec(memory_space=pl.ANY)

C = 32
T = 9
KL = 64
ROWS = 16
LANES = 128
EXT = ROWS + 8
SLOTS = EXT + 2
SCALE = 1.0 / math.sqrt(T * T * C)
READY = ((0, 8), (8, 16), (16, 20), (20, 26))
STEPS = (7, 11, 13, 15)
RUNS = (
    ((0, 4, 0), (4, 8, 4)),
    ((8, 12, 8), (12, 16, 16)),
    ((16, 18, 12), (18, 20, 20)),
    ((20, 22, 14), (22, 24, 22), (24, 25, -1), (25, 26, -2)),
)
PLACE = [0] * EXT
for _runs in RUNS:
    for _low, _high, _row in _runs:
        for _n in range(_high - _low):
            if _row >= 0:
                PLACE[_row + _n] = _low + _n
PARTS = ((0, 12), (12, 19), (19, 27))
LAST = (16, 23)
FIELD = 19


def spot(row):
    return row + 3 if row < 8 else row + 11 if row < 16 else row - 5


GROUP = 3


def split(x):
    hi = x.astype(BF16)
    return hi, (x - hi.astype(F32)).astype(BF16)


def lane_index(rows):
    return lax.broadcasted_iota(jnp.int32, (rows, LANES), 1)


def roll(x, shift):
    return pltpu.roll(x, shift % LANES, 1) if shift % LANES else x


def inside(lane, shift):
    return lane >= shift if shift > 0 else lane < LANES + shift


def synthesis(codes, ws, zbuf, acc, part, ready):
    owners = part.shape[0]
    share = C // owners
    lane = lane_index(C)
    zero_rows = jnp.zeros((3 * KL, 2 * LANES), BF16)
    zbuf[0 : 3 * KL] = zero_rows
    zbuf[9 * 3 * KL : 10 * 3 * KL] = zero_rows
    for t in range(8):
        hi, lo = split(jnp.concatenate([codes[t], codes[t + 8]], axis=1))
        base = (t + 1) * 3 * KL
        zbuf[base : base + KL] = hi
        zbuf[base + KL : base + 2 * KL] = lo
        zbuf[base + 2 * KL : base + 3 * KL] = hi
    rims = [jnp.zeros((C, LANES), F32), jnp.zeros((C, LANES), F32)]

    def put(slot, row):
        for q in range(owners):
            part[q, slot] = row[q * share : (q + 1) * share]

    for ho in range(16):
        first, last = max(0, 8 - ho) // 2, min(8, 15 - ho) // 2
        depth = (last - first + 1) * 6 * KL
        start = (2 * first + ho - 7) * 3 * KL
        taps = jnp.dot(
            ws[:, first * 6 * KL : first * 6 * KL + depth],
            zbuf[start : start + depth],
            preferred_element_type=F32,
        )
        for half in range(2):
            main = jnp.zeros((C, LANES), F32)
            rim = jnp.zeros((C, LANES), F32)
            for b in range(T):
                moved = roll(taps[b * C : (b + 1) * C, half * LANES : (half + 1) * LANES], 4 - b)
                if b == 4:
                    main = main + moved
                else:
                    keep = inside(lane, 4 - b)
                    main = main + jnp.where(keep, moved, 0.0)
                    rim = rim + jnp.where(keep, 0.0, moved)
            row = ho + 8 * half
            rims[row // 16] = rims[row // 16] + roll(rim, 8 * (row % 16) + 4)
            if half == 0 and ho >= 8:
                main = main + acc[ho - 8]
            if half == 1 and ho < 8:
                acc[ho] = main
            else:
                put(PLACE[row], main)
        if ho in STEPS[:-1]:
            ready(STEPS.index(ho))
    put(24, rims[0])
    put(25, rims[1])
    ready(len(STEPS) - 1)


def gathered(err, slot):
    return jnp.concatenate([err[q, slot] for q in range(err.shape[0])], axis=0)


def error_row(err, row, fix):
    main = gathered(err, spot(row))
    if 8 <= row < 16:
        lane = lane_index(C)
        ends = (lane < 4) | (lane >= LANES - 4)
        main = main + jnp.where(ends, roll(fix, -(8 * row + 4)), 0.0)
    return main


def adjoint_step(err, arrived, wa, level, codes, ebuf, hbuf, qbuf, qbuf2, gbuf):
    wide = 3 * C
    lane_c = lane_index(C)
    lane = lane_index(KL)
    place = lane % 8
    arrived(0)
    rims = [gathered(err, 0), gathered(err, 1)]
    for t in range(T):
        hi, lo = split(
            jnp.where(lane_c < LANES - 8 * t, roll(rims[0], -8 * t), roll(rims[1], -8 * t))
        )
        hbuf[t * wide : t * wide + C] = hi
        hbuf[t * wide + C : t * wide + 2 * C] = lo
        hbuf[t * wide + 2 * C : t * wide + 3 * C] = hi
    qbuf[:, 0:LANES] = jnp.dot(wa[:, 0 : T * wide], hbuf[...], preferred_element_type=F32)
    edge = jnp.zeros((KL, LANES), F32)
    for b in range(T):
        s = b - 4
        if s == 0:
            continue
        keep = (place >= 4) & (place < 4 + s) if s > 0 else (place < 4) & (place >= 4 + s)
        edge = edge + jnp.where(keep, roll(qbuf[b * KL : (b + 1) * KL, 0:LANES], s), 0.0)
    gbuf[...] = edge

    def take(first, last):
        fix = gathered(err, 2)
        for row in range(first, last + 1):
            hi, lo = split(error_row(err, row, fix))
            for t, side in ((row, 0), (row - 8, 1)):
                if 0 <= t < 16:
                    cols = slice(side * LANES, (side + 1) * LANES)
                    ebuf[t * wide : t * wide + C, cols] = hi
                    ebuf[t * wide + C : t * wide + 2 * C, cols] = lo
                    ebuf[t * wide + 2 * C : t * wide + 3 * C, cols] = hi

    arrived(2)
    take(0, LAST[0])
    ends = (lane < 4) | (lane >= LANES - 4)

    def multiply(i, out):
        start = pl.multiple_of(i * wide, wide)
        out[...] = jnp.dot(
            wa[:, 0 : T * wide], ebuf[pl.ds(start, T * wide)], preferred_element_type=F32
        )

    def shrink(i, taps):
        bound = level[...]
        for half in range(2):
            row = i + 8 * half
            back = LANES - 4 - 64 * half - 8 * i
            total = jnp.where(ends, pltpu.roll(gbuf[...], back, 1), 0.0)
            for b in range(T):
                moved = roll(taps[b * KL : (b + 1) * KL, half * LANES : (half + 1) * LANES], b - 4)
                if b != 4:
                    moved = jnp.where(inside(lane, b - 4), moved, 0.0)
                total = total + moved
            shifted = codes[row] - (ETA_CODE * SCALE) * total
            codes[row] = shifted - jnp.clip(shifted, -bound, bound)

    def two(n, carry):
        multiply(2 * n + 1, qbuf2)
        shrink(2 * n, qbuf)
        multiply(2 * n + 2, qbuf)
        shrink(2 * n + 1, qbuf2)
        return carry

    multiply(0, qbuf)
    arrived(1)
    take(LAST[0] + 1, LAST[1])
    lax.fori_loop(0, 3, two, 0)
    multiply(7, qbuf2)
    shrink(6, qbuf)
    shrink(7, qbuf2)


def stacked_codes(codes, cbuf):
    wide = 3 * LANES
    none = jnp.zeros((KL, wide), BF16)
    for i in range(-2, ROWS + 2):
        inner = 0 <= i < ROWS
        if inner:
            hi, lo = split(codes[i])
        for n in range(GROUP):
            u = i + 2 - n
            if not 0 <= u < ROWS + 2:
                continue
            rows = slice(n * KL, (n + 1) * KL)
            if inner:
                cbuf[rows, u * wide : u * wide + LANES] = hi
                cbuf[rows, u * wide + LANES : u * wide + 2 * LANES] = lo
                cbuf[rows, u * wide + 2 * LANES : u * wide + 3 * LANES] = hi
            else:
                cbuf[rows, u * wide : (u + 1) * wide] = none


def shifted_errors(err, arrived, lbuf, first, last):
    lane = lane_index(C)
    if first == 0:
        arrived(0)
        arrived(2)
    fix = gathered(err, 2)
    rims = [gathered(err, 0), gathered(err, 1)]
    for row in range(first, last):
        if row - 1 == LAST[0]:
            arrived(1)
        main = error_row(err, row, fix)
        rim = roll(rims[row // 16], -(8 * (row % 16) + 4))
        for b in range(T):
            s = b - 4
            if s > 0:
                field = jnp.where(lane >= LANES - s, rim, main)
            elif s < 0:
                field = jnp.where(lane < -s, rim, main)
            else:
                field = main
            hi, lo = split(roll(field, s))
            at = row * 3 * LANES
            lbuf[b * C : (b + 1) * C, at : at + LANES] = hi
            lbuf[b * C : (b + 1) * C, at + LANES : at + 2 * LANES] = hi
            lbuf[b * C : (b + 1) * C, at + 2 * LANES : at + 3 * LANES] = lo


def correlation(group, lbuf, cbuf, gacc, parts):
    first, depth = group * GROUP, (ROWS + 2) * 3 * LANES
    start = (6 - first) * 3 * LANES
    gacc[0 : T * C, 0 : GROUP * KL] = lax.dot_general(
        lbuf[:, start : start + depth],
        cbuf[...],
        (((1,), (1,)), ((), ())),
        preferred_element_type=F32,
    )
    groups, share = parts.shape[1], parts.shape[3]
    for m in range(0, 2 * LANES, LANES):
        for n in range(0, 3 * LANES, LANES):
            turned = jnp.transpose(gacc[n : n + LANES, m : m + LANES])
            width = min(LANES, T * C - n)
            for k in range(0, min(LANES, GROUP * KL - m), share):
                a, block = first + (m + k) // KL, (k % KL) // share
                parts[block % 2, block // 2, a, :, n : n + width] = turned[k : k + share, :width]


def synthesis_weights(atoms, ws, taken):
    for a in range(0, T + 1, 2):
        pairs = []
        for t in (a, a + 1):
            if t < T:
                taken(t)
                field = jnp.concatenate([atoms[t, b] for b in range(T)], axis=0)
                hi, lo = split(field)
                pairs += [hi.astype(F32), hi.astype(F32), lo.astype(F32)]
            else:
                pairs += [jnp.zeros((T * C, KL), F32)] * 3
        for n in range(3):
            lanes = slice(a * 3 * KL + n * LANES, a * 3 * KL + (n + 1) * LANES)
            ws[:, lanes] = jnp.concatenate(pairs[2 * n : 2 * n + 2], axis=1).astype(BF16)


def adjoint_weights(atoms, flip, wa):
    depth = flip.shape[0]
    flip[T * 3 * C : depth] = jnp.zeros((depth - T * 3 * C, flip.shape[1]), F32)
    flip[:, T * KL :] = jnp.zeros((depth, flip.shape[1] - T * KL), F32)
    for a in range(T):
        at = (T - 1 - a) * 3 * C
        for b in range(0, T, 2):
            cols = slice(b * KL, min(b + 2, T) * KL)
            field = atoms[a, b]
            if b + 1 < T:
                field = jnp.concatenate([field, atoms[a, b + 1]], axis=1)
            hi, lo = split(field)
            flip[at : at + C, cols] = hi.astype(F32)
            flip[at + C : at + 2 * C, cols] = hi.astype(F32)
            flip[at + 2 * C : at + 3 * C, cols] = lo.astype(F32)
    for m in range(0, flip.shape[1], LANES):
        rows = min(LANES, T * KL - m)
        for n in range(0, depth, LANES):
            turned = jnp.transpose(flip[n : n + LANES, m : m + LANES])
            wa[m : m + rows, n : n + LANES] = turned[:rows].astype(BF16)


def owned_atoms(atoms, start, share, own):
    row = lax.broadcasted_iota(jnp.int32, (16, KL), 0)
    col = lax.broadcasted_iota(jnp.int32, (16, KL), 1)
    pick = jnp.where(col == row + start, 1.0, 0.0).astype(BF16)
    for a in range(T):
        field = jnp.concatenate([atoms[a, b] for b in range(T)], axis=0)
        hi, rest = field.astype(BF16), None
        rest = field - hi.astype(F32)
        mid = rest.astype(BF16)
        low = (rest - mid.astype(F32)).astype(BF16)
        total = None
        for piece in (hi, mid, low):
            part = lax.dot_general(
                pick, piece, (((1,), (1,)), ((), ())), preferred_element_type=F32
            )
            total = part if total is None else total + part
        own[a] = total[:share]


def greet(peers):
    barrier = pltpu.get_barrier_semaphore()
    for peer in peers:
        pl.semaphore_signal(barrier, inc=1, device_id=peer, device_id_type=MESH)


def greeted(peers):
    pl.semaphore_wait(pltpu.get_barrier_semaphore(), len(peers))


def remote(src, dst, sems, peer):
    return pltpu.make_async_remote_copy(
        src_ref=src,
        dst_ref=dst,
        send_sem=sems.at[0],
        recv_sem=sems.at[1],
        device_id=peer,
        device_id_type=MESH,
    )


def send(src, dst, sems, peer):
    remote(src, dst, sems, peer).start()


class Grid:
    def __init__(self, owners, rows, cols):
        self.owners, self.rows, self.cols, self.halves = owners, rows, cols, cols // 2
        self.q, self.r, self.c = (lax.axis_index(n) for n in ("atom", "row", "col"))
        q, r, c = self.q, self.r, self.c
        self.core, self.z = lax.rem(c, 2), lax.div(c, 2)
        self.peers = [{"atom": lax.rem(q + d, owners)} for d in range(1, owners)]
        self.up, self.down = {"row": lax.rem(r + rows - 1, rows)}, {"row": lax.rem(r + 1, rows)}
        self.left, self.right = {"col": lax.rem(c + cols - 1, cols)}, {"col": lax.rem(c + 1, cols)}
        self.partner = {"col": 2 * self.z + 1 - self.core}
        self.blocks = []
        for dr in range(rows):
            for dz in range(self.halves):
                if dr + dz > 0:
                    pr, pz = lax.rem(r + dr, rows), lax.rem(self.z + dz, self.halves)
                    place = {"row": pr, "col": 2 * pz + self.core}
                    self.blocks.append((pr * self.halves + pz, place))
        self.corners = [{**v, **h} for v in (self.up, self.down) for h in (self.left, self.right)]
        self.everyone = self.peers + [self.left, self.right] + [p for _, p in self.blocks]
        self.everyone += self.corners


def send_sums(grid, u, n, chunk):
    low, high = READY[chunk]
    for d, p in enumerate(grid.peers):
        source = u["part"].at[p["atom"], low:high]
        send(source, u["rbuf"].at[n, d, low:high], u["s_rs"].at[n, chunk], p)


def all_of(ref, sems, peer):
    return remote(ref, ref, sems, peer)


def meet(grid, u, n):
    share, rows, cols = C // grid.owners, grid.rows, grid.cols
    piece, field, image = u["piece"], u["field"], u["image"]
    rim, msg, err = u["rim"].at[n], u["msg"], u["err"].at[n]
    h1, h2, h3 = rim.at[0:18], rim.at[18:22], rim.at[22:26]
    someone = grid.partner
    part, rbuf = u["part"], u["rbuf"].at[n]
    lane = lane_index(share)
    ends = (lane < 4) | (lane >= LANES - 4)
    low = lane % 8 < 4
    packed = [jnp.zeros((share, LANES), F32), jnp.zeros((share, LANES), F32)]
    for chunk, runs in enumerate(RUNS):
        first, last = READY[chunk]
        all_of(rbuf.at[:, first:last], u["s_rs"].at[n, chunk], someone).wait_recv()
        for begin, end, row in runs:
            total = part[grid.q, begin:end]
            for d in range(grid.owners - 1):
                total = total + rbuf[d, begin:end]
            total = total * SCALE
            if 4 <= row < 4 + ROWS:
                total = total - image[row - 4 : row - 4 + end - begin]
            at = row + 1 if row >= 0 else (0 if row == -1 else SLOTS - 1)
            piece[at : at + end - begin] = total
            for k in range(end - begin if row >= 0 else 0):
                edge = jnp.where(ends, total[k], 0.0)
                packed[(row + k) // 16] += roll(edge, 8 * ((row + k) % 16) + 4)

    s_rim = u["s_rim"].at[n]
    send(piece.at[17:26], h1.at[0:9], s_rim, grid.down)
    send(piece.at[0:9], h1.at[9:18], s_rim, grid.up)
    f_up, f_down = (grid.r > 0).astype(F32), (grid.r < rows - 1).astype(F32)
    f_left, f_right = (grid.c > 0).astype(F32), (grid.c < cols - 1).astype(F32)
    own = [piece[0], piece[SLOTS - 1]]
    for v in range(2):
        msg[v] = jnp.where(low, packed[v], own[v])
        msg[2 + v] = jnp.where(low, own[v], packed[v])
    send(msg.at[1], h3.at[0], s_rim, grid.corners[3])
    send(msg.at[0], h3.at[1], s_rim, grid.corners[1])
    send(msg.at[3], h3.at[2], s_rim, grid.corners[2])
    send(msg.at[2], h3.at[3], s_rim, grid.corners[0])
    send(msg.at[0:2], h2.at[0:2], s_rim, grid.right)
    send(msg.at[2:4], h2.at[2:4], s_rim, grid.left)
    first, last = PARTS[2]
    for p in grid.peers:
        send(piece.at[9:17], err.at[grid.q, first:last], u["s_ag"].at[n, 2], p)
    err[grid.q, first:last] = piece[9:17]
    all_of(rim, s_rim, someone).wait_recv()
    begin = lane < 64
    sides = []
    for side, factor in ((0, f_left), (1, f_right)):
        above = h3[2 * side] * f_up
        below = jnp.where(begin, h3[2 * side + 1], 0.0) * f_down
        sides.append([(h2[2 * side] + above) * factor, (h2[2 * side + 1] + below) * factor])
    rims = [own[0] + h1[8] * f_up, own[1] + jnp.where(begin, h1[9], 0.0) * f_down]
    inner = [None, None]
    for v in range(2):
        from_left, from_right = sides[0][v], sides[1][v]
        rims[v] = rims[v] + jnp.where(low, from_left, from_right)
        inner[v] = jnp.where(low, from_right, from_left)
        rims[v] = rims[v] * jnp.where(low, f_left, f_right)
    field[0] = rims[0] * jnp.where(lane < 32, f_up, 1.0)
    field[1] = jnp.where(begin, rims[1] * jnp.where(lane >= 32, f_down, 1.0), 0.0)
    field[2] = inner[0]
    for row in (*range(8), *range(16, EXT)):
        fix = roll(inner[row // 16], -(8 * (row % 16) + 4))
        value = piece[row + 1]
        if row < 8:
            value = value + h1[row] * f_up
        if row >= 16:
            value = value + h1[row - 6] * f_down
        value = value + jnp.where(ends, fix, 0.0)
        if row < 4:
            value = value * f_up
        if row >= EXT - 4:
            value = value * f_down
        field[spot(row)] = value
        if row in LAST:
            chunk = LAST.index(row)
            first, last = PARTS[chunk]
            for p in grid.peers:
                send(field.at[first:last], err.at[grid.q, first:last], u["s_ag"].at[n, chunk], p)
            err[grid.q, first:last] = field[first:last]
    for chunk, (first, last) in enumerate(READY):
        all_of(rbuf.at[:, first:last], u["s_rs"].at[n, chunk], someone).wait_send()
    all_of(rim, s_rim, someone).wait_send()

    def arrived(chunk):
        first, last = PARTS[chunk]
        all_of(rbuf.at[:, 0 : last - first], u["s_ag"].at[n, chunk], someone).wait_recv()
        if chunk == 1:
            for other, (first, last) in enumerate(PARTS):
                all_of(rbuf.at[:, 0 : last - first], u["s_ag"].at[n, other], someone).wait_send()

    return arrived


def kernel(sizes, names, owned, image, warm, atoms, limits, new_codes, grad, picked, *scratch):
    u = dict(zip(names, scratch))
    grid = Grid(*sizes)
    share = C // grid.owners
    greet(grid.everyone)
    codes = u["codes"]
    loads = [
        pltpu.make_async_copy(atoms.at[a], u["atoms"].at[a], u["s_atoms"].at[a]) for a in range(T)
    ]
    for load in loads:
        load.start()
    for i in range(ROWS):
        pltpu.make_async_copy(warm.at[:, i], codes.at[i], u["s_in"].at[1]).start()
    for i in range(ROWS):
        bands = image.at[pl.ds(grid.q * share, share), i]
        pltpu.make_async_copy(bands, u["image"].at[i], u["s_in"].at[2]).start()
    diagonal = lax.broadcasted_iota(jnp.int32, (KL, KL), 0) == lax.broadcasted_iota(
        jnp.int32, (KL, KL), 1
    )
    column = jnp.sum(jnp.where(diagonal, limits[...], 0.0), axis=1, keepdims=True)
    u["level"][...] = jnp.broadcast_to(ETA_CODE * column, (KL, LANES))
    synthesis_weights(u["atoms"], u["ws"], lambda a: loads[a].wait())
    pltpu.make_async_copy(codes, codes, u["s_in"].at[1]).wait()
    pltpu.make_async_copy(u["image"], u["image"], u["s_in"].at[2]).wait()

    def partial_sums(n, begin):
        def ready(chunk):
            if chunk == 0:
                begin()
            send_sums(grid, u, n, chunk)

        synthesis(codes, u["ws"], u["zbuf"], u["acc"], u["part"], ready)

    partial_sums(0, lambda: greeted(grid.everyone))
    adjoint_weights(u["atoms"], u["flip"], u["wa"])
    owned_atoms(u["atoms"], (grid.r * grid.cols + grid.c) * owned, owned, picked)

    def one(n, carry):
        arrived = meet(grid, u, n)
        buffers = [u[s] for s in ("ebuf", "hbuf", "qbuf", "qbuf2", "gbuf")]
        adjoint_step(u["err"].at[n], arrived, u["wa"], u["level"], codes, *buffers)
        partial_sums(n + 1, lambda: None)
        return carry

    lax.fori_loop(0, ITERS, one, 0)
    for i in range(ROWS):
        pltpu.make_async_copy(codes.at[i], new_codes.at[:, i], u["s_in"].at[3]).start()
    stacked_codes(codes, u["cbuf"])
    arrived = meet(grid, u, ITERS)
    err, lbuf = u["err"].at[ITERS], u["lbuf"]
    parts, half, total, chunks = (u[s] for s in ("parts", "half", "total", "chunks"))

    def taps(group):
        return slice(group * GROUP, (group + 1) * GROUP)

    def spread(group):
        at, s_core = taps(group), u["s_core"].at[group]
        all_of(half.at[:, at], s_core, grid.partner).wait_recv()
        total[:, at] = parts[grid.core, :, at] + half[:, at]
        for d, (g, p) in enumerate(grid.blocks):
            send(total.at[g, at], chunks.at[d, at], u["s_block"].at[group], p)

    def correlate(group):
        correlation(group, lbuf, u["cbuf"], u["gacc"], parts)
        at = taps(group)
        send(parts.at[1 - grid.core, :, at], half.at[:, at], u["s_core"].at[group], grid.partner)

    shifted_errors(err, arrived, lbuf, 0, 18)
    correlate(2)
    shifted_errors(err, arrived, lbuf, 18, EXT)
    correlate(1)
    spread(2)
    correlate(0)
    spread(1)
    spread(0)
    pixels = ROWS * LANES * grid.rows * grid.cols
    for group in (2, 1, 0):
        at = taps(group)
        all_of(chunks.at[:, at], u["s_block"].at[group], grid.partner).wait_recv()
        summed = total[grid.r * grid.halves + grid.z, at]
        for d in range(len(grid.blocks)):
            summed = summed + chunks[d, at]
        grad[at] = summed * (1.0 / pixels)
    for group in range(T // GROUP):
        at = taps(group)
        all_of(half.at[:, at], u["s_core"].at[group], grid.partner).wait_send()
        all_of(chunks.at[:, at], u["s_block"].at[group], grid.partner).wait_send()
    pltpu.make_async_copy(codes, codes, u["s_in"].at[3]).wait()


def finish(codes, grad, own, velocity, new_codes, new_atoms, new_velocity, buffer, sems):
    pieces = [pl.ds(n * (KL // 4), KL // 4) for n in range(4)]
    reads = [
        pltpu.make_async_copy(codes.at[at], buffer.at[at], sems.at[0, n])
        for n, at in enumerate(pieces)
    ]
    writes = [
        pltpu.make_async_copy(buffer.at[at], new_codes.at[at], sems.at[1, n])
        for n, at in enumerate(pieces)
    ]
    for read in reads:
        read.start()
    for read, write in zip(reads, writes):
        read.wait()
        write.start()
    square = None
    for b in range(T):
        cols = slice(b * C, (b + 1) * C)
        fresh = MOMENTUM * velocity[:, b] + grad[:, :, cols]
        stepped = own[:, :, cols] - LEARN_RATE * fresh
        new_velocity[:, b] = fresh
        new_atoms[:, b] = stepped
        term = jnp.sum(stepped * stepped, axis=0)
        square = term if square is None else square + term
    square = jnp.sum(square, axis=1, keepdims=True) * (1.0 / (T * T * C))
    gain = lax.rsqrt(square + EPSILON)
    for b in range(T):
        new_atoms[:, b] = new_atoms[:, b] * gain[None]
    for write in writes:
        write.wait()


def struct(shape, dtype=F32):
    return jax.ShapeDtypeStruct(shape, dtype)


def shards(hyper_image, warm_codes, dictionary, thresholds, velocity):
    owners, rows, cols = lax.axis_size("atom"), lax.axis_size("row"), lax.axis_size("col")
    share, owned, halves = C // owners, velocity.shape[0], cols // 2
    rounds, groups = ITERS + 1, rows * halves
    piece = pltpu.VMEM((SLOTS, share, LANES), F32)
    chunk = (T, owned, T * C)
    sems = pltpu.SemaphoreType.DMA
    scratch = {
        "codes": pltpu.VMEM((ROWS, KL, LANES), F32),
        "atoms": pltpu.VMEM((T, T, C, KL), F32),
        "image": pltpu.VMEM((ROWS, share, LANES), F32),
        "level": pltpu.VMEM((KL, LANES), F32),
        "ws": pltpu.VMEM((T * C, (T + 1) * 3 * KL), BF16),
        "flip": pltpu.VMEM((7 * LANES, 5 * LANES), F32),
        "wa": pltpu.VMEM((T * KL, 7 * LANES), BF16),
        "zbuf": pltpu.VMEM((10 * 3 * KL, 2 * LANES), BF16),
        "acc": pltpu.VMEM((8, C, LANES), F32),
        "part": pltpu.VMEM((owners, SLOTS, share, LANES), F32),
        "err": pltpu.VMEM((rounds, owners, FIELD + 8, share, LANES), F32),
        "rbuf": pltpu.VMEM((rounds, owners - 1, SLOTS, share, LANES), F32),
        "piece": piece,
        "rim": pltpu.VMEM((rounds, 26, share, LANES), F32),
        "msg": pltpu.VMEM((4, share, LANES), F32),
        "field": pltpu.VMEM((FIELD, share, LANES), F32),
        "ebuf": pltpu.VMEM((16 * 3 * C, 2 * LANES), BF16),
        "hbuf": pltpu.VMEM((T * 3 * C, LANES), BF16),
        "qbuf": pltpu.VMEM((T * KL, 2 * LANES), F32),
        "qbuf2": pltpu.VMEM((T * KL, 2 * LANES), F32),
        "gbuf": pltpu.VMEM((KL, LANES), F32),
        "lbuf": pltpu.VMEM((T * C, EXT * 3 * LANES), BF16),
        "cbuf": pltpu.VMEM((GROUP * KL, (ROWS + 2) * 3 * LANES), BF16),
        "gacc": pltpu.VMEM((3 * LANES, 2 * LANES), F32),
        "parts": pltpu.VMEM((2, groups) + chunk, F32),
        "half": pltpu.VMEM((groups,) + chunk, F32),
        "total": pltpu.VMEM((groups,) + chunk, F32),
        "chunks": pltpu.VMEM((groups - 1,) + chunk, F32),
        "s_in": sems((4,)),
        "s_atoms": sems((T,)),
        "s_rs": sems((rounds, len(READY), 2)),
        "s_rim": sems((rounds, 2)),
        "s_ag": sems((rounds, len(PARTS), 2)),
        "s_core": sems((T // GROUP, 2)),
        "s_block": sems((T // GROUP, 2)),
    }
    natural = (T, T, owned, C)
    codes, grad, own = pl.pallas_call(
        functools.partial(kernel, (owners, rows, cols), tuple(scratch), owned),
        out_shape=(struct((KL, ROWS, LANES)), struct(chunk), struct(chunk)),
        in_specs=[ANY, ANY, ANY, VMEM],
        out_specs=(ANY, VMEM, VMEM),
        scratch_shapes=list(scratch.values()),
        compiler_params=pltpu.CompilerParams(
            vmem_limit_bytes=60 << 20, collective_id=0, has_side_effects=True
        ),
    )(hyper_image, warm_codes, dictionary.transpose(1, 2, 3, 0), thresholds.reshape(1, KL))
    new_codes, new_atoms, new_velocity = pl.pallas_call(
        finish,
        out_shape=(struct((KL, ROWS, LANES)), struct(natural), struct(natural)),
        in_specs=[ANY, VMEM, VMEM, VMEM],
        out_specs=(ANY, VMEM, VMEM),
        scratch_shapes=[pltpu.VMEM((KL, ROWS, LANES), F32), sems((2, 4))],
    )(codes, grad, own, velocity.transpose(1, 2, 0, 3))
    return new_codes, new_atoms.transpose(2, 0, 1, 3), new_velocity.transpose(2, 0, 1, 3)


def solution(mesh):
    in_specs = (
        P(None, "row", "col"),
        P("atom", "row", "col"),
        P("atom", None, None, None),
        P("atom"),
        P(("atom", "row", "col"), None, None, None),
    )
    out_specs = (
        P("atom", "row", "col"),
        P(("atom", "row", "col"), None, None, None),
        P(("atom", "row", "col"), None, None, None),
    )
    return jax.shard_map(shards, mesh=mesh, in_specs=in_specs, out_specs=out_specs, check_vma=False)
```

```python
import functools
import math

import jax
import jax.numpy as jnp
from jax import lax
from jax.experimental import pallas as pl
from jax.experimental.pallas import tpu as pltpu
from jax.sharding import PartitionSpec as P

ITERS = 2
ETA_CODE = 0.05
MOMENTUM = 0.9
LEARN_RATE = 200.0
EPSILON = 1e-06

F32 = jnp.float32
BF16 = jnp.bfloat16
MESH = pl.DeviceIdType.MESH
VMEM = pl.BlockSpec(memory_space=pltpu.VMEM)
ANY = pl.BlockSpec(memory_space=pl.ANY)

C = 32
T = 9
KL = 64
ROWS = 16
LANES = 128
EXT = ROWS + 8
SLOTS = EXT + 2
SCALE = 1.0 / math.sqrt(T * T * C)
READY = ((0, 8), (8, 16), (16, 20), (20, 26))
STEPS = (7, 11, 13, 15)
RUNS = (
    ((0, 4, 0), (4, 8, 4)),
    ((8, 12, 8), (12, 16, 16)),
    ((16, 18, 12), (18, 20, 20)),
    ((20, 22, 14), (22, 24, 22), (24, 25, -1), (25, 26, -2)),
)
PLACE = [0] * EXT
for _runs in RUNS:
    for _low, _high, _row in _runs:
        for _n in range(_high - _low):
            if _row >= 0:
                PLACE[_row + _n] = _low + _n
PARTS = ((0, 12), (12, 19), (19, 27))
LAST = (16, 23)
FIELD = 19


def spot(row):
    return row + 3 if row < 8 else row + 11 if row < 16 else row - 5


GROUP = 3


def split(x):
    hi = x.astype(BF16)
    return hi, (x - hi.astype(F32)).astype(BF16)


def lane_index(rows):
    return lax.broadcasted_iota(jnp.int32, (rows, LANES), 1)


def roll(x, shift):
    return pltpu.roll(x, shift % LANES, 1) if shift % LANES else x


def inside(lane, shift):
    return lane >= shift if shift > 0 else lane < LANES + shift


def synthesis(codes, ws, zbuf, acc, part, ready):
    owners = part.shape[0]
    share = C // owners
    lane = lane_index(C)
    zero_rows = jnp.zeros((3 * KL, 2 * LANES), BF16)
    zbuf[0 : 3 * KL] = zero_rows
    zbuf[9 * 3 * KL : 10 * 3 * KL] = zero_rows
    for t in range(8):
        hi, lo = split(jnp.concatenate([codes[t], codes[t + 8]], axis=1))
        base = (t + 1) * 3 * KL
        zbuf[base : base + KL] = hi
        zbuf[base + KL : base + 2 * KL] = lo
        zbuf[base + 2 * KL : base + 3 * KL] = hi
    rims = [jnp.zeros((C, LANES), F32), jnp.zeros((C, LANES), F32)]

    def put(slot, row):
        for q in range(owners):
            part[q, slot] = row[q * share : (q + 1) * share]

    for ho in range(16):
        first, last = max(0, 8 - ho) // 2, min(8, 15 - ho) // 2
        depth = (last - first + 1) * 6 * KL
        start = (2 * first + ho - 7) * 3 * KL
        taps = jnp.dot(
            ws[:, first * 6 * KL : first * 6 * KL + depth],
            zbuf[start : start + depth],
            preferred_element_type=F32,
        )
        for half in range(2):
            main = jnp.zeros((C, LANES), F32)
            rim = jnp.zeros((C, LANES), F32)
            for b in range(T):
                moved = roll(taps[b * C : (b + 1) * C, half * LANES : (half + 1) * LANES], 4 - b)
                if b == 4:
                    main = main + moved
                else:
                    keep = inside(lane, 4 - b)
                    main = main + jnp.where(keep, moved, 0.0)
                    rim = rim + jnp.where(keep, 0.0, moved)
            row = ho + 8 * half
            rims[row // 16] = rims[row // 16] + roll(rim, 8 * (row % 16) + 4)
            if half == 0 and ho >= 8:
                main = main + acc[ho - 8]
            if half == 1 and ho < 8:
                acc[ho] = main
            else:
                put(PLACE[row], main)
        if ho in STEPS[:-1]:
            ready(STEPS.index(ho))
    put(24, rims[0])
    put(25, rims[1])
    ready(len(STEPS) - 1)


def gathered(err, slot):
    return jnp.concatenate([err[q, slot] for q in range(err.shape[0])], axis=0)


def error_row(err, row, fix):
    main = gathered(err, spot(row))
    if 8 <= row < 16:
        lane = lane_index(C)
        ends = (lane < 4) | (lane >= LANES - 4)
        main = main + jnp.where(ends, roll(fix, -(8 * row + 4)), 0.0)
    return main


def adjoint_step(err, arrived, wa, level, codes, ebuf, hbuf, qbuf, qbuf2, gbuf):
    wide = 3 * C
    lane_c = lane_index(C)
    lane = lane_index(KL)
    place = lane % 8
    arrived(0)
    rims = [gathered(err, 0), gathered(err, 1)]
    for t in range(T):
        hi, lo = split(
            jnp.where(lane_c < LANES - 8 * t, roll(rims[0], -8 * t), roll(rims[1], -8 * t))
        )
        hbuf[t * wide : t * wide + C] = hi
        hbuf[t * wide + C : t * wide + 2 * C] = lo
        hbuf[t * wide + 2 * C : t * wide + 3 * C] = hi
    qbuf[:, 0:LANES] = jnp.dot(wa[:, 0 : T * wide], hbuf[...], preferred_element_type=F32)
    edge = jnp.zeros((KL, LANES), F32)
    for b in range(T):
        s = b - 4
        if s == 0:
            continue
        keep = (place >= 4) & (place < 4 + s) if s > 0 else (place < 4) & (place >= 4 + s)
        edge = edge + jnp.where(keep, roll(qbuf[b * KL : (b + 1) * KL, 0:LANES], s), 0.0)
    gbuf[...] = edge

    def take(first, last):
        fix = gathered(err, 2)
        for row in range(first, last + 1):
            hi, lo = split(error_row(err, row, fix))
            for t, side in ((row, 0), (row - 8, 1)):
                if 0 <= t < 16:
                    cols = slice(side * LANES, (side + 1) * LANES)
                    ebuf[t * wide : t * wide + C, cols] = hi
                    ebuf[t * wide + C : t * wide + 2 * C, cols] = lo
                    ebuf[t * wide + 2 * C : t * wide + 3 * C, cols] = hi

    arrived(2)
    take(0, LAST[0])
    ends = (lane < 4) | (lane >= LANES - 4)

    def multiply(i, out):
        start = pl.multiple_of(i * wide, wide)
        out[...] = jnp.dot(
            wa[:, 0 : T * wide], ebuf[pl.ds(start, T * wide)], preferred_element_type=F32
        )

    def shrink(i, taps):
        bound = level[...]
        for half in range(2):
            row = i + 8 * half
            back = LANES - 4 - 64 * half - 8 * i
            total = jnp.where(ends, pltpu.roll(gbuf[...], back, 1), 0.0)
            for b in range(T):
                moved = roll(taps[b * KL : (b + 1) * KL, half * LANES : (half + 1) * LANES], b - 4)
                if b != 4:
                    moved = jnp.where(inside(lane, b - 4), moved, 0.0)
                total = total + moved
            shifted = codes[row] - (ETA_CODE * SCALE) * total
            codes[row] = shifted - jnp.clip(shifted, -bound, bound)

    def two(n, carry):
        multiply(2 * n + 1, qbuf2)
        shrink(2 * n, qbuf)
        multiply(2 * n + 2, qbuf)
        shrink(2 * n + 1, qbuf2)
        return carry

    multiply(0, qbuf)
    arrived(1)
    take(LAST[0] + 1, LAST[1])
    lax.fori_loop(0, 3, two, 0)
    multiply(7, qbuf2)
    shrink(6, qbuf)
    shrink(7, qbuf2)


def stacked_codes(codes, cbuf):
    wide = 3 * LANES
    none = jnp.zeros((KL, wide), BF16)
    for i in range(-2, ROWS + 2):
        inner = 0 <= i < ROWS
        if inner:
            hi, lo = split(codes[i])
        for n in range(GROUP):
            u = i + 2 - n
            if not 0 <= u < ROWS + 2:
                continue
            rows = slice(n * KL, (n + 1) * KL)
            if inner:
                cbuf[rows, u * wide : u * wide + LANES] = hi
                cbuf[rows, u * wide + LANES : u * wide + 2 * LANES] = lo
                cbuf[rows, u * wide + 2 * LANES : u * wide + 3 * LANES] = hi
            else:
                cbuf[rows, u * wide : (u + 1) * wide] = none


def shifted_errors(err, arrived, lbuf, first, last):
    lane = lane_index(C)
    if first == 0:
        arrived(0)
        arrived(2)
    fix = gathered(err, 2)
    rims = [gathered(err, 0), gathered(err, 1)]
    for row in range(first, last):
        if row - 1 == LAST[0]:
            arrived(1)
        main = error_row(err, row, fix)
        rim = roll(rims[row // 16], -(8 * (row % 16) + 4))
        for b in range(T):
            s = b - 4
            if s > 0:
                field = jnp.where(lane >= LANES - s, rim, main)
            elif s < 0:
                field = jnp.where(lane < -s, rim, main)
            else:
                field = main
            hi, lo = split(roll(field, s))
            at = row * 3 * LANES
            lbuf[b * C : (b + 1) * C, at : at + LANES] = hi
            lbuf[b * C : (b + 1) * C, at + LANES : at + 2 * LANES] = hi
            lbuf[b * C : (b + 1) * C, at + 2 * LANES : at + 3 * LANES] = lo


def correlation(group, lbuf, cbuf, gacc, parts):
    first, depth = group * GROUP, (ROWS + 2) * 3 * LANES
    start = (6 - first) * 3 * LANES
    gacc[0 : T * C, 0 : GROUP * KL] = lax.dot_general(
        lbuf[:, start : start + depth],
        cbuf[...],
        (((1,), (1,)), ((), ())),
        preferred_element_type=F32,
    )
    groups, share = parts.shape[1], parts.shape[3]
    for m in range(0, 2 * LANES, LANES):
        for n in range(0, 3 * LANES, LANES):
            turned = jnp.transpose(gacc[n : n + LANES, m : m + LANES])
            width = min(LANES, T * C - n)
            for k in range(0, min(LANES, GROUP * KL - m), share):
                a, block = first + (m + k) // KL, (k % KL) // share
                parts[block % 2, block // 2, a, :, n : n + width] = turned[k : k + share, :width]


def synthesis_weights(atoms, ws, taken):
    for a in range(0, T + 1, 2):
        pairs = []
        for t in (a, a + 1):
            if t < T:
                taken(t)
                field = jnp.concatenate([atoms[t, b] for b in range(T)], axis=0)
                hi, lo = split(field)
                pairs += [hi.astype(F32), hi.astype(F32), lo.astype(F32)]
            else:
                pairs += [jnp.zeros((T * C, KL), F32)] * 3
        for n in range(3):
            lanes = slice(a * 3 * KL + n * LANES, a * 3 * KL + (n + 1) * LANES)
            ws[:, lanes] = jnp.concatenate(pairs[2 * n : 2 * n + 2], axis=1).astype(BF16)


def adjoint_weights(atoms, flip, wa):
    depth = flip.shape[0]
    flip[T * 3 * C : depth] = jnp.zeros((depth - T * 3 * C, flip.shape[1]), F32)
    flip[:, T * KL :] = jnp.zeros((depth, flip.shape[1] - T * KL), F32)
    for a in range(T):
        at = (T - 1 - a) * 3 * C
        for b in range(0, T, 2):
            cols = slice(b * KL, min(b + 2, T) * KL)
            field = atoms[a, b]
            if b + 1 < T:
                field = jnp.concatenate([field, atoms[a, b + 1]], axis=1)
            hi, lo = split(field)
            flip[at : at + C, cols] = hi.astype(F32)
            flip[at + C : at + 2 * C, cols] = hi.astype(F32)
            flip[at + 2 * C : at + 3 * C, cols] = lo.astype(F32)
    for m in range(0, flip.shape[1], LANES):
        rows = min(LANES, T * KL - m)
        for n in range(0, depth, LANES):
            turned = jnp.transpose(flip[n : n + LANES, m : m + LANES])
            wa[m : m + rows, n : n + LANES] = turned[:rows].astype(BF16)


def owned_atoms(atoms, start, share, own):
    row = lax.broadcasted_iota(jnp.int32, (16, KL), 0)
    col = lax.broadcasted_iota(jnp.int32, (16, KL), 1)
    pick = jnp.where(col == row + start, 1.0, 0.0).astype(BF16)
    for a in range(T):
        field = jnp.concatenate([atoms[a, b] for b in range(T)], axis=0)
        hi, rest = field.astype(BF16), None
        rest = field - hi.astype(F32)
        mid = rest.astype(BF16)
        low = (rest - mid.astype(F32)).astype(BF16)
        total = None
        for piece in (hi, mid, low):
            part = lax.dot_general(
                pick, piece, (((1,), (1,)), ((), ())), preferred_element_type=F32
            )
            total = part if total is None else total + part
        own[a] = total[:share]


def greet(peers):
    barrier = pltpu.get_barrier_semaphore()
    for peer in peers:
        pl.semaphore_signal(barrier, inc=1, device_id=peer, device_id_type=MESH)


def greeted(peers):
    pl.semaphore_wait(pltpu.get_barrier_semaphore(), len(peers))


def remote(src, dst, sems, peer):
    return pltpu.make_async_remote_copy(
        src_ref=src,
        dst_ref=dst,
        send_sem=sems.at[0],
        recv_sem=sems.at[1],
        device_id=peer,
        device_id_type=MESH,
    )


def send(src, dst, sems, peer):
    remote(src, dst, sems, peer).start()


class Grid:
    def __init__(self, owners, rows, cols):
        self.owners, self.rows, self.cols, self.halves = owners, rows, cols, cols // 2
        self.q, self.r, self.c = (lax.axis_index(n) for n in ("atom", "row", "col"))
        q, r, c = self.q, self.r, self.c
        self.core, self.z = lax.rem(c, 2), lax.div(c, 2)
        self.peers = [{"atom": lax.rem(q + d, owners)} for d in range(1, owners)]
        self.up, self.down = {"row": lax.rem(r + rows - 1, rows)}, {"row": lax.rem(r + 1, rows)}
        self.left, self.right = {"col": lax.rem(c + cols - 1, cols)}, {"col": lax.rem(c + 1, cols)}
        self.partner = {"col": 2 * self.z + 1 - self.core}
        self.blocks = []
        for dr in range(rows):
            for dz in range(self.halves):
                if dr + dz > 0:
                    pr, pz = lax.rem(r + dr, rows), lax.rem(self.z + dz, self.halves)
                    place = {"row": pr, "col": 2 * pz + self.core}
                    self.blocks.append((pr * self.halves + pz, place))
        self.corners = [{**v, **h} for v in (self.up, self.down) for h in (self.left, self.right)]
        self.everyone = self.peers + [self.left, self.right] + [p for _, p in self.blocks]
        self.everyone += self.corners


def send_sums(grid, u, n, chunk):
    low, high = READY[chunk]
    for d, p in enumerate(grid.peers):
        source = u["part"].at[p["atom"], low:high]
        send(source, u["rbuf"].at[n, d, low:high], u["s_rs"].at[n, chunk], p)


def all_of(ref, sems, peer):
    return remote(ref, ref, sems, peer)


def meet(grid, u, n):
    share, rows, cols = C // grid.owners, grid.rows, grid.cols
    piece, field, image = u["piece"], u["field"], u["image"]
    rim, msg, err = u["rim"].at[n], u["msg"], u["err"].at[n]
    h1, h2, h3 = rim.at[0:18], rim.at[18:22], rim.at[22:26]
    someone = grid.partner
    part, rbuf = u["part"], u["rbuf"].at[n]
    lane = lane_index(share)
    ends = (lane < 4) | (lane >= LANES - 4)
    low = lane % 8 < 4
    packed = [jnp.zeros((share, LANES), F32), jnp.zeros((share, LANES), F32)]
    for chunk, runs in enumerate(RUNS):
        first, last = READY[chunk]
        all_of(rbuf.at[:, first:last], u["s_rs"].at[n, chunk], someone).wait_recv()
        for begin, end, row in runs:
            total = part[grid.q, begin:end]
            for d in range(grid.owners - 1):
                total = total + rbuf[d, begin:end]
            total = total * SCALE
            if 4 <= row < 4 + ROWS:
                total = total - image[row - 4 : row - 4 + end - begin]
            at = row + 1 if row >= 0 else (0 if row == -1 else SLOTS - 1)
            piece[at : at + end - begin] = total
            for k in range(end - begin if row >= 0 else 0):
                edge = jnp.where(ends, total[k], 0.0)
                packed[(row + k) // 16] += roll(edge, 8 * ((row + k) % 16) + 4)

    s_rim = u["s_rim"].at[n]
    f_up, f_down = (grid.r > 0).astype(F32), (grid.r < rows - 1).astype(F32)
    f_left, f_right = (grid.c > 0).astype(F32), (grid.c < cols - 1).astype(F32)
    own = [piece[0], piece[SLOTS - 1]]
    for v in range(2):
        msg[v] = jnp.where(low, packed[v], own[v])
        msg[2 + v] = jnp.where(low, own[v], packed[v])
    send(msg.at[1], h3.at[0], s_rim, grid.corners[3])
    send(msg.at[0], h3.at[1], s_rim, grid.corners[1])
    send(msg.at[3], h3.at[2], s_rim, grid.corners[2])
    send(msg.at[2], h3.at[3], s_rim, grid.corners[0])
    send(msg.at[0:2], h2.at[0:2], s_rim, grid.right)
    send(msg.at[2:4], h2.at[2:4], s_rim, grid.left)
    send(piece.at[17:26], h1.at[0:9], s_rim, grid.down)
    send(piece.at[0:9], h1.at[9:18], s_rim, grid.up)
    first, last = PARTS[2]
    for p in grid.peers:
        send(piece.at[9:17], err.at[grid.q, first:last], u["s_ag"].at[n, 2], p)
    err[grid.q, first:last] = piece[9:17]
    all_of(rim, s_rim, someone).wait_recv()
    begin = lane < 64
    sides = []
    for side, factor in ((0, f_left), (1, f_right)):
        above = h3[2 * side] * f_up
        below = jnp.where(begin, h3[2 * side + 1], 0.0) * f_down
        sides.append([(h2[2 * side] + above) * factor, (h2[2 * side + 1] + below) * factor])
    rims = [own[0] + h1[8] * f_up, own[1] + jnp.where(begin, h1[9], 0.0) * f_down]
    inner = [None, None]
    for v in range(2):
        from_left, from_right = sides[0][v], sides[1][v]
        rims[v] = rims[v] + jnp.where(low, from_left, from_right)
        inner[v] = jnp.where(low, from_right, from_left)
        rims[v] = rims[v] * jnp.where(low, f_left, f_right)
    field[0] = rims[0] * jnp.where(lane < 32, f_up, 1.0)
    field[1] = jnp.where(begin, rims[1] * jnp.where(lane >= 32, f_down, 1.0), 0.0)
    field[2] = inner[0]
    for row in (*range(8), *range(16, EXT)):
        fix = roll(inner[row // 16], -(8 * (row % 16) + 4))
        value = piece[row + 1]
        if row < 8:
            value = value + h1[row] * f_up
        if row >= 16:
            value = value + h1[row - 6] * f_down
        value = value + jnp.where(ends, fix, 0.0)
        if row < 4:
            value = value * f_up
        if row >= EXT - 4:
            value = value * f_down
        field[spot(row)] = value
        if row in LAST:
            chunk = LAST.index(row)
            first, last = PARTS[chunk]
            for p in grid.peers:
                send(field.at[first:last], err.at[grid.q, first:last], u["s_ag"].at[n, chunk], p)
            err[grid.q, first:last] = field[first:last]
    for chunk, (first, last) in enumerate(READY):
        all_of(rbuf.at[:, first:last], u["s_rs"].at[n, chunk], someone).wait_send()
    all_of(rim, s_rim, someone).wait_send()

    def arrived(chunk):
        first, last = PARTS[chunk]
        all_of(rbuf.at[:, 0 : last - first], u["s_ag"].at[n, chunk], someone).wait_recv()
        if chunk == 1:
            for other, (first, last) in enumerate(PARTS):
                all_of(rbuf.at[:, 0 : last - first], u["s_ag"].at[n, other], someone).wait_send()

    return arrived


def kernel(sizes, names, owned, image, warm, atoms, limits, new_codes, grad, picked, *scratch):
    u = dict(zip(names, scratch))
    grid = Grid(*sizes)
    share = C // grid.owners
    greet(grid.everyone)
    codes = u["codes"]
    loads = [
        pltpu.make_async_copy(atoms.at[a], u["atoms"].at[a], u["s_atoms"].at[a]) for a in range(T)
    ]
    for load in loads:
        load.start()
    for i in range(ROWS):
        pltpu.make_async_copy(warm.at[:, i], codes.at[i], u["s_in"].at[1]).start()
    for i in range(ROWS):
        bands = image.at[pl.ds(grid.q * share, share), i]
        pltpu.make_async_copy(bands, u["image"].at[i], u["s_in"].at[2]).start()
    diagonal = lax.broadcasted_iota(jnp.int32, (KL, KL), 0) == lax.broadcasted_iota(
        jnp.int32, (KL, KL), 1
    )
    column = jnp.sum(jnp.where(diagonal, limits[...], 0.0), axis=1, keepdims=True)
    u["level"][...] = jnp.broadcast_to(ETA_CODE * column, (KL, LANES))
    synthesis_weights(u["atoms"], u["ws"], lambda a: loads[a].wait())
    pltpu.make_async_copy(codes, codes, u["s_in"].at[1]).wait()
    pltpu.make_async_copy(u["image"], u["image"], u["s_in"].at[2]).wait()

    def partial_sums(n, begin):
        def ready(chunk):
            if chunk == 0:
                begin()
            send_sums(grid, u, n, chunk)

        synthesis(codes, u["ws"], u["zbuf"], u["acc"], u["part"], ready)

    partial_sums(0, lambda: greeted(grid.everyone))
    adjoint_weights(u["atoms"], u["flip"], u["wa"])
    owned_atoms(u["atoms"], (grid.r * grid.cols + grid.c) * owned, owned, picked)

    def one(n, carry):
        arrived = meet(grid, u, n)
        buffers = [u[s] for s in ("ebuf", "hbuf", "qbuf", "qbuf2", "gbuf")]
        adjoint_step(u["err"].at[n], arrived, u["wa"], u["level"], codes, *buffers)
        partial_sums(n + 1, lambda: None)
        return carry

    lax.fori_loop(0, ITERS, one, 0)
    for i in range(ROWS):
        pltpu.make_async_copy(codes.at[i], new_codes.at[:, i], u["s_in"].at[3]).start()
    stacked_codes(codes, u["cbuf"])
    arrived = meet(grid, u, ITERS)
    err, lbuf = u["err"].at[ITERS], u["lbuf"]
    parts, half, total, chunks = (u[s] for s in ("parts", "half", "total", "chunks"))

    def taps(group):
        return slice(group * GROUP, (group + 1) * GROUP)

    def spread(group):
        at, s_core = taps(group), u["s_core"].at[group]
        all_of(half.at[:, at], s_core, grid.partner).wait_recv()
        total[:, at] = parts[grid.core, :, at] + half[:, at]
        for d, (g, p) in enumerate(grid.blocks):
            send(total.at[g, at], chunks.at[d, at], u["s_block"].at[group], p)

    def correlate(group):
        correlation(group, lbuf, u["cbuf"], u["gacc"], parts)
        at = taps(group)
        send(parts.at[1 - grid.core, :, at], half.at[:, at], u["s_core"].at[group], grid.partner)

    shifted_errors(err, arrived, lbuf, 0, 18)
    correlate(2)
    shifted_errors(err, arrived, lbuf, 18, EXT)
    correlate(1)
    spread(2)
    correlate(0)
    spread(1)
    spread(0)
    pixels = ROWS * LANES * grid.rows * grid.cols
    for group in (2, 1, 0):
        at = taps(group)
        all_of(chunks.at[:, at], u["s_block"].at[group], grid.partner).wait_recv()
        summed = total[grid.r * grid.halves + grid.z, at]
        for d in range(len(grid.blocks)):
            summed = summed + chunks[d, at]
        grad[at] = summed * (1.0 / pixels)
    for group in range(T // GROUP):
        at = taps(group)
        all_of(half.at[:, at], u["s_core"].at[group], grid.partner).wait_send()
        all_of(chunks.at[:, at], u["s_block"].at[group], grid.partner).wait_send()
    pltpu.make_async_copy(codes, codes, u["s_in"].at[3]).wait()


def finish(codes, grad, own, velocity, new_codes, new_atoms, new_velocity, buffer, sems):
    pieces = [pl.ds(n * (KL // 4), KL // 4) for n in range(4)]
    reads = [
        pltpu.make_async_copy(codes.at[at], buffer.at[at], sems.at[0, n])
        for n, at in enumerate(pieces)
    ]
    writes = [
        pltpu.make_async_copy(buffer.at[at], new_codes.at[at], sems.at[1, n])
        for n, at in enumerate(pieces)
    ]
    for read in reads:
        read.start()
    for read, write in zip(reads, writes):
        read.wait()
        write.start()
    square = None
    for b in range(T):
        cols = slice(b * C, (b + 1) * C)
        fresh = MOMENTUM * velocity[:, b] + grad[:, :, cols]
        stepped = own[:, :, cols] - LEARN_RATE * fresh
        new_velocity[:, b] = fresh
        new_atoms[:, b] = stepped
        term = jnp.sum(stepped * stepped, axis=0)
        square = term if square is None else square + term
    square = jnp.sum(square, axis=1, keepdims=True) * (1.0 / (T * T * C))
    gain = lax.rsqrt(square + EPSILON)
    for b in range(T):
        new_atoms[:, b] = new_atoms[:, b] * gain[None]
    for write in writes:
        write.wait()


def struct(shape, dtype=F32):
    return jax.ShapeDtypeStruct(shape, dtype)


def shards(hyper_image, warm_codes, dictionary, thresholds, velocity):
    owners, rows, cols = lax.axis_size("atom"), lax.axis_size("row"), lax.axis_size("col")
    share, owned, halves = C // owners, velocity.shape[0], cols // 2
    rounds, groups = ITERS + 1, rows * halves
    piece = pltpu.VMEM((SLOTS, share, LANES), F32)
    chunk = (T, owned, T * C)
    sems = pltpu.SemaphoreType.DMA
    scratch = {
        "codes": pltpu.VMEM((ROWS, KL, LANES), F32),
        "atoms": pltpu.VMEM((T, T, C, KL), F32),
        "image": pltpu.VMEM((ROWS, share, LANES), F32),
        "level": pltpu.VMEM((KL, LANES), F32),
        "ws": pltpu.VMEM((T * C, (T + 1) * 3 * KL), BF16),
        "flip": pltpu.VMEM((7 * LANES, 5 * LANES), F32),
        "wa": pltpu.VMEM((T * KL, 7 * LANES), BF16),
        "zbuf": pltpu.VMEM((10 * 3 * KL, 2 * LANES), BF16),
        "acc": pltpu.VMEM((8, C, LANES), F32),
        "part": pltpu.VMEM((owners, SLOTS, share, LANES), F32),
        "err": pltpu.VMEM((rounds, owners, FIELD + 8, share, LANES), F32),
        "rbuf": pltpu.VMEM((rounds, owners - 1, SLOTS, share, LANES), F32),
        "piece": piece,
        "rim": pltpu.VMEM((rounds, 26, share, LANES), F32),
        "msg": pltpu.VMEM((4, share, LANES), F32),
        "field": pltpu.VMEM((FIELD, share, LANES), F32),
        "ebuf": pltpu.VMEM((16 * 3 * C, 2 * LANES), BF16),
        "hbuf": pltpu.VMEM((T * 3 * C, LANES), BF16),
        "qbuf": pltpu.VMEM((T * KL, 2 * LANES), F32),
        "qbuf2": pltpu.VMEM((T * KL, 2 * LANES), F32),
        "gbuf": pltpu.VMEM((KL, LANES), F32),
        "lbuf": pltpu.VMEM((T * C, EXT * 3 * LANES), BF16),
        "cbuf": pltpu.VMEM((GROUP * KL, (ROWS + 2) * 3 * LANES), BF16),
        "gacc": pltpu.VMEM((3 * LANES, 2 * LANES), F32),
        "parts": pltpu.VMEM((2, groups) + chunk, F32),
        "half": pltpu.VMEM((groups,) + chunk, F32),
        "total": pltpu.VMEM((groups,) + chunk, F32),
        "chunks": pltpu.VMEM((groups - 1,) + chunk, F32),
        "s_in": sems((4,)),
        "s_atoms": sems((T,)),
        "s_rs": sems((rounds, len(READY), 2)),
        "s_rim": sems((rounds, 2)),
        "s_ag": sems((rounds, len(PARTS), 2)),
        "s_core": sems((T // GROUP, 2)),
        "s_block": sems((T // GROUP, 2)),
    }
    natural = (T, T, owned, C)
    codes, grad, own = pl.pallas_call(
        functools.partial(kernel, (owners, rows, cols), tuple(scratch), owned),
        out_shape=(struct((KL, ROWS, LANES)), struct(chunk), struct(chunk)),
        in_specs=[ANY, ANY, ANY, VMEM],
        out_specs=(ANY, VMEM, VMEM),
        scratch_shapes=list(scratch.values()),
        compiler_params=pltpu.CompilerParams(
            vmem_limit_bytes=60 << 20, collective_id=0, has_side_effects=True
        ),
    )(hyper_image, warm_codes, dictionary.transpose(1, 2, 3, 0), thresholds.reshape(1, KL))
    new_codes, new_atoms, new_velocity = pl.pallas_call(
        finish,
        out_shape=(struct((KL, ROWS, LANES)), struct(natural), struct(natural)),
        in_specs=[ANY, VMEM, VMEM, VMEM],
        out_specs=(ANY, VMEM, VMEM),
        scratch_shapes=[pltpu.VMEM((KL, ROWS, LANES), F32), sems((2, 4))],
    )(codes, grad, own, velocity.transpose(1, 2, 0, 3))
    return new_codes, new_atoms.transpose(2, 0, 1, 3), new_velocity.transpose(2, 0, 1, 3)


def solution(mesh):
    in_specs = (
        P(None, "row", "col"),
        P("atom", "row", "col"),
        P("atom", None, None, None),
        P("atom"),
        P(("atom", "row", "col"), None, None, None),
    )
    out_specs = (
        P("atom", "row", "col"),
        P(("atom", "row", "col"), None, None, None),
        P(("atom", "row", "col"), None, None, None),
    )
    return jax.shard_map(shards, mesh=mesh, in_specs=in_specs, out_specs=out_specs, check_vma=False)
```
